256 devices in a mesh: track: 4 (over x_hi, core), tile: 64 (over z, y, x_lo).
Axes of the slice: x: 4 (x_hi: 2, x_lo: 2; x = x_hi * 2 + x_lo), y: 4, z: 8, core: 2. Of those that a mesh axis runs over, the one named last changes fastest.
Arguments:
- displacement: float32 [4, 5120, 1024], P('track', 'tile'), may hold values from -6 to 6
- velocity: float32 [4, 5120, 1024], P('track', 'tile'), may hold values from -3 to 3
- seasonal: float32 [2, 4, 5120, 1024], P(None, 'track', 'tile'), may hold values from -3 to 3
- cov_diag: float32 [4, 4, 5120, 1024], P(None, 'track', 'tile'), may hold values from 0.05 to 1
- cov_corr: float32 [6, 4, 5120, 1024], P(None, 'track', 'tile'), may hold values from -0.3 to 0.3
- observed: float32 [4, 5120, 1024], P('track', 'tile'), may hold values from -9 to 9
- noise_var: float32 [4, 5120, 1024], P('track', 'tile'), may hold values from 0.1 to 1
- coherence: float32 [4, 5120, 1024], P('track', 'tile'), may hold values from 0.2 to 1
- valid: int32 [4, 5120, 1024], P('track', 'tile'), may hold values 0 or 1
- screen_operator: bfloat16 [4, 5120, 5120], P('track', None, 'tile'), may hold values from -0.25 to 0.25
- process_noise: float32 [4], replicated, may hold values from 0.05 to 0.5
- track_scene: int32 [4], P('track'), may hold values from 0 to 15
- scene_interval: float32 [16], replicated, may hold values from 0.5 to 2
- margin_up: int32 [4, 64, 40], P('track', 'tile'), may hold values from -1 to 639, as said below
- margin_down: int32 [4, 64, 40], P('track', 'tile'), may hold values from -1 to 632, as said below
Outputs:
- new_state: float32 [4, 4, 5120, 1024], P(None, 'track', 'tile')
- new_cov: float32 [10, 4, 5120, 1024], P(None, 'track', 'tile')
The draws below stay inside these ranges and needn't reach their ends.
Inputs may be any that keep to these rules, and one draw needn't show every extreme that they name: Slot j of margin_up at track t and tile k and slot j of margin_down at track t + 1 and tile k name blocks of the same ground; one is -1 (empty) exactly where the other is. margin_up names blocks of the last 128 columns, margin_down of the first 128; non-empty entries of one list are distinct; the last track's margin_up and the first track's margin_down are empty; for every pair of tracks some tile has all 40 slots filled. `margin_down`: see margin_up.
All inputs are finite; a program needn't handle non-finite values. No bound on the sum of `valid` on one device may be relied on, other than what follows from the above.
Results may differ from the reference program's by a relative error of at most 0.0014.
Values may be sent and summed in bfloat16 or wider, within the bound.
No kernel may reach another device: no remote copies, remote signals or barrier semaphores. Data moves between devices by JAX's collectives and lax.ppermute only.
A program may use at most 64 MiB of HBM per device.

```python
import math
from functools import reduce
import jax
import jax.numpy as jnp
from jax import lax

R_DEV = 80
W = 1024
ACQS = 16
TRACKS = 4
TILES = 64
ROWS = 5120
NB = 40
QC = 32
CB = 8


def margin_lists(key):
    key = jax.random.fold_in(key, 11)
    key_count, key_full, key_up, key_down = jax.random.split(key, 4)
    pair_count = TRACKS - 1
    counts = jax.random.randint(key_count, (pair_count, TILES), max(NB // 4, 1), NB + 1)
    full_tile = jax.random.randint(key_full, (pair_count,), 0, TILES)
    is_full = jnp.arange(TILES)[None, :] == full_tile[:, None]
    counts = jnp.where(is_full, NB, counts)
    last_row = jnp.arange(R_DEV) == R_DEV - 1

    def row_order(key_rows):
        scores = jax.random.randint(key_rows, (pair_count, TILES, R_DEV), 0, 1 << 20) * R_DEV + jnp.arange(R_DEV)[None, None, :]
        scores = jnp.where(is_full[:, :, None] & last_row[None, None, :], -1, scores)
        return jnp.argsort(scores, axis=2, stable=True)[:, :, :NB].astype(jnp.int32)
    is_live = jnp.arange(NB)[None, None, :] < counts[:, :, None]
    column_blocks = W // 128
    up_pairs = jnp.where(is_live, row_order(key_up) * column_blocks + column_blocks - 1, -1)
    down_pairs = jnp.where(is_live, row_order(key_down) * column_blocks, -1)
    empty_rows = jnp.full((1, TILES, NB), -1, jnp.int32)
    upper = jnp.concatenate([up_pairs.astype(jnp.int32), empty_rows], axis=0)
    lower = jnp.concatenate([empty_rows, down_pairs.astype(jnp.int32)], axis=0)
    return (upper, lower)


def draw_margin_up(key, part):
    return margin_lists(key)[0]


def draw_margin_down(key, part):
    return margin_lists(key)[1]


def set_ends(array, rng, smallest, largest):
    dims = array.shape
    place = [jax.random.randint(jax.random.fold_in(rng, axis), (), 0, dims[axis]) for axis in range(len(dims))]
    array = array.at[tuple(place)].set(smallest)
    longest = dims.index(max(dims))
    place[longest] = (place[longest] + 1) % dims[longest]
    return array.at[tuple(place)].set(largest)


def strengthened(array, key, source, target, blocks, factor):
    def block_of(axis_at):
        return (jnp.arange(array.shape[axis_at]) // (array.shape[axis_at] // blocks)).reshape((-1,) + (1,) * (array.ndim - 1 - axis_at))

    near = jax.random.permutation(key, blocks)[block_of(target)]
    far = (block_of(target) + blocks // 2) % blocks
    return jnp.where((block_of(source) == near) | (block_of(source) == far), factor * array, array)


def level_of(key, dims, cuts, least, top_value):
    factor_of, own = 1.0, jax.random.fold_in(key, 6)
    for axis_at, blocks in cuts:
        steps = jnp.exp(jax.random.uniform(jax.random.fold_in(own, axis_at), (blocks,), jnp.float32, least / len(cuts), top_value / len(cuts)))
        factor_of = factor_of * jnp.repeat(steps, dims[axis_at] // blocks).reshape([-1 if axis == axis_at else 1 for axis in range(len(dims))])
    return factor_of


def normal_values(key, shape, scale, reach, pieces=(), dtype=jnp.bfloat16):
    gain = level_of(key, shape, pieces, -0.22, 0.18) if pieces else 1.0
    entries = jax.random.normal(key, shape, jnp.float32) * scale * gain
    return jnp.minimum(jnp.maximum(entries, -reach), reach).astype(dtype)


def noise_with(stream_key, extent, scale, most, cuts, heavy, held_as=jnp.bfloat16):
    drawn = scale * jax.random.normal(stream_key, extent, jnp.float32)
    if cuts:
        drawn = drawn * level_of(stream_key, extent, cuts, -0.22, 0.18)
    return jnp.clip(strengthened(drawn, jax.random.fold_in(stream_key, 3), *heavy), -most, most).astype(held_as)


def setup_inputs(seed: int = 0) -> dict:
    keys = jax.random.split(jax.random.key(seed), 16)
    displacement = normal_values(keys[0], (TRACKS, ROWS, W), 1.0, 6.0, ((0, 4), (1, 64)), jnp.float32)
    velocity = normal_values(keys[1], (TRACKS, ROWS, W), 0.5, 3.0, ((0, 4), (1, 64)), jnp.float32)
    seasonal = normal_values(keys[2], (2, TRACKS, ROWS, W), 0.5, 3.0, ((1, 4), (2, 64)), jnp.float32)
    cov_diag = jnp.clip(jnp.exp(math.log(1.0) - 2.9957323 * jax.random.uniform(keys[3], (4, TRACKS, ROWS, W), jnp.float32) ** level_of(keys[3], (4, TRACKS, ROWS, W), ((1, 4), (2, 64)), -0.2, 0.2)), 0.05, 1.0)
    cov_corr = jnp.clip(jax.random.uniform(keys[4], (6, TRACKS, ROWS, W), jnp.float32, -0.3, 0.3) * level_of(keys[4], (6, TRACKS, ROWS, W), ((1, 4), (2, 64)), -0.4, 0.0), -0.3, 0.3)
    observed = normal_values(keys[5], (TRACKS, ROWS, W), 1.5, 9.0, ((0, 4), (1, 64)), jnp.float32)
    noise_var = jnp.clip(jnp.exp(math.log(1.0) - 2.3025851 * jax.random.uniform(keys[6], (TRACKS, ROWS, W), jnp.float32) ** level_of(keys[6], (TRACKS, ROWS, W), ((0, 4), (1, 64)), -0.2, 0.2)), 0.1, 1.0)
    coherence = jnp.clip(0.2 + 0.8 * jax.random.uniform(keys[7], (TRACKS, ROWS, W), jnp.float32) ** level_of(keys[7], (TRACKS, ROWS, W), ((0, 4), (1, 64)), -0.2, 0.2), 0.2, 1.0)
    valid = set_ends((jax.random.randint(keys[8], (TRACKS, ROWS, W), 0, 4) < 3).astype(jnp.int32), jax.random.fold_in(keys[8], 1), 0, 1)
    screen_operator = noise_with(keys[9], (TRACKS, ROWS, ROWS), ROWS ** -0.5, 0.25, ((0, 4), (2, 64)), (2, 1, 64, 4.0))
    process_noise = jnp.clip(jnp.exp(jax.random.uniform(keys[10], (4,), jnp.float32, math.log(0.05), math.log(0.5))), 0.05, 0.5)
    track_scene = set_ends(jax.random.randint(keys[11], (TRACKS,), 0, ACQS), jax.random.fold_in(keys[11], 1), 0, ACQS - 1).astype(jnp.int32)
    scene_interval = jnp.clip(jax.random.uniform(keys[12], (ACQS,), jnp.float32, 0.5, 2.0), 0.5, 2.0)
    margin_up = draw_margin_up(jax.random.fold_in(keys[15], 71), 0)
    margin_down = draw_margin_down(jax.random.fold_in(keys[15], 71), 0)
    return dict(displacement=displacement, velocity=velocity, seasonal=seasonal, cov_diag=cov_diag, cov_corr=cov_corr, observed=observed, noise_var=noise_var, coherence=coherence, valid=valid, screen_operator=screen_operator, process_noise=process_noise, track_scene=track_scene, scene_interval=scene_interval, margin_up=margin_up, margin_down=margin_down)


SEASON_RATE = 2.0 * math.pi * 12.0 / 365.25
ALONG_COEF = 0.2
ACROSS_COEF = 0.1
WEIGHT_FLOOR = 0.1
BLOCK_SCALE = 0.25
PAIR_LIST = ((0, 1), (0, 2), (0, 3), (1, 2), (1, 3), (2, 3))

def add_all(items):
    return reduce(lambda a, b: a + b, items)

def predict(state_now, cov_diag, cov_corr, interval, process_noise):
    deviation = [jnp.sqrt(cov_diag[i]) for i in range(4)]
    covariance = [[None] * 4 for i in range(4)]
    for i in range(4):
        covariance[i][i] = cov_diag[i]
    for n, (i, j) in enumerate(PAIR_LIST):
        covariance[i][j] = cov_corr[n] * deviation[i] * deviation[j]
        covariance[j][i] = covariance[i][j]
    rotate_cos = jnp.cos(SEASON_RATE * interval)
    rotate_sin = jnp.sin(SEASON_RATE * interval)
    transition = [[1.0, interval, None, None], [None, 1.0, None, None], [None, None, rotate_cos, -rotate_sin], [None, None, rotate_sin, rotate_cos]]
    state_pred = [add_all([transition[i][k] * state_now[k] for k in range(4) if transition[i][k] is not None]) for i in range(4)]
    left_product = [[add_all([transition[i][k] * covariance[k][j] for k in range(4) if transition[i][k] is not None]) for j in range(4)] for i in range(4)]
    pred_cov = [[add_all([left_product[i][k] * transition[j][k] for k in range(4) if transition[j][k] is not None]) for j in range(4)] for i in range(4)]
    for i in range(4):
        pred_cov[i][i] = pred_cov[i][i] + process_noise[i] * interval
    return (state_pred, pred_cov)

def update(state_pred, pred_cov, innovation, noise_var, coherence, valid_mask):
    cross_cov = [pred_cov[i][0] + pred_cov[i][2] for i in range(4)]
    variance = cross_cov[0] + cross_cov[2] + noise_var / coherence
    new_state = [state_pred[i] + valid_mask * (cross_cov[i] / variance) * innovation for i in range(4)]
    diag_out = [pred_cov[i][i] - valid_mask * cross_cov[i] * cross_cov[i] / variance for i in range(4)]
    pair_out = [pred_cov[i][j] - valid_mask * cross_cov[i] * cross_cov[j] / variance for i, j in PAIR_LIST]
    return (jnp.stack(new_state), jnp.stack(diag_out + pair_out))

def pick_one(block_data, index_list):
    safe_index = jnp.where(index_list >= 0, index_list, 0)
    keep_mask = (index_list >= 0).astype(jnp.float32)
    return block_data[:, safe_index] * keep_mask[None, :, None]

def place_one(index_list, row_data, block_count):
    safe_index = jnp.where(index_list >= 0, index_list, block_count)
    blank = jnp.zeros((row_data.shape[0], block_count, row_data.shape[2]), jnp.float32)
    return blank.at[:, safe_index].add(row_data, mode='drop')

def reference(displacement, velocity, seasonal, cov_diag, cov_corr, observed, noise_var, coherence, valid, screen_operator, process_noise, track_scene, scene_interval, margin_up, margin_down):
    onehot = (jnp.arange(ACQS)[None, :] == track_scene[:, None]).astype(jnp.float32)
    interval = lax.optimization_barrier(jnp.sum(onehot * scene_interval[None, :], axis=1))[:, None, None]
    state_now = [displacement, velocity, seasonal[0], seasonal[1]]
    state_pred, pred_cov = predict(state_now, cov_diag, cov_corr, interval, process_noise)
    valid_mask = valid.astype(jnp.float32)
    weight = coherence * valid_mask
    innovation_raw = observed - (state_pred[0] + state_pred[2])
    block_sums = (lax.optimization_barrier(jnp.sum((weight * innovation_raw).reshape(TRACKS, ROWS, QC, 32), axis=3)) * BLOCK_SCALE).astype(jnp.bfloat16)
    screen = jnp.stack([jnp.dot(screen_operator[t], block_sums[t], preferred_element_type=jnp.float32) for t in range(TRACKS)])
    cleaned = innovation_raw - jnp.repeat(screen, 32, axis=2)
    padded = jnp.pad(cleaned, ((0, 0), (1, 1), (1, 1)))
    smooth = cleaned + ALONG_COEF * (padded[:, :-2, 1:-1] + padded[:, 2:, 1:-1] - 2.0 * cleaned) + ACROSS_COEF * (padded[:, 1:-1, :-2] + padded[:, 1:-1, 2:] - 2.0 * cleaned)
    block_count = R_DEV * CB
    payload = jnp.stack([(weight * smooth).reshape(TRACKS, TILES, block_count, 128), weight.reshape(TRACKS, TILES, block_count, 128)])
    pick_tiles = jax.vmap(pick_one, in_axes=(1, 0), out_axes=1)
    place_tiles = jax.vmap(lambda a, b: place_one(a, b, block_count), in_axes=(0, 1), out_axes=1)
    received = jnp.zeros_like(payload)
    for t in range(TRACKS - 1):
        lower_send = pick_tiles(payload[:, t], margin_up[t])
        upper_send = pick_tiles(payload[:, t + 1], margin_down[t + 1])
        received = received.at[:, t + 1].add(place_tiles(margin_down[t + 1], lower_send))
        received = received.at[:, t].add(place_tiles(margin_up[t], upper_send))
    received_wv = received[0].reshape(TRACKS, ROWS, W)
    received_w = received[1].reshape(TRACKS, ROWS, W)
    innovation = ((weight + WEIGHT_FLOOR) * smooth + received_wv) / (weight + WEIGHT_FLOOR + received_w)
    return update(state_pred, pred_cov, innovation, noise_var, coherence, valid_mask)
```

```python
import functools
import math

import jax
import jax.numpy as jnp
from jax import lax
from jax.experimental import pallas as pl
from jax.experimental.pallas import tpu as pltpu
from jax.sharding import PartitionSpec as P

SEASON_RATE = 2.0 * math.pi * 12.0 / 365.25
ALONG_COEF = 0.2
ACROSS_COEF = 0.1
WEIGHT_FLOOR = 0.1
BLOCK_SCALE = 0.25
PAIR_LIST = ((0, 1), (0, 2), (0, 3), (1, 2), (1, 3), (2, 3))

R = 80
W = 1024
PAD = 8
WIN = R + 2 * PAD
SUB = WIN // 4
NB = 40
F32 = jnp.float32
BF16 = jnp.bfloat16

SMEM = pl.BlockSpec(memory_space=pltpu.SMEM)
VMEM = pl.BlockSpec(memory_space=pltpu.VMEM)
ANY = pl.BlockSpec(memory_space=pl.ANY)


def scene_terms(scene, table):
    interval = table[scene[0]]
    angle = jnp.full((1, 1), SEASON_RATE * interval, F32)
    return interval, jnp.cos(angle), jnp.sin(angle)


def front_kernel(
    tiles,
    scene,
    table,
    d_h,
    v_h,
    s_h,
    o_h,
    c_h,
    m_h,
    op_h,
    raw_ref,
    part_ref,
    ea_ref,
    eb_ref,
    buf,
    mbuf,
    opbuf,
    sums,
    prod,
    sems,
    op_sem,
):
    half = R // 2
    rows_all = tiles * R
    copies = []
    for i in range(2):
        rows = pl.ds(i * half, half)
        sources = [d_h.at[0], v_h.at[0], s_h.at[0, 0], s_h.at[1, 0], o_h.at[0], c_h.at[0]]
        group = [
            pltpu.make_async_copy(src.at[rows], buf.at[n, rows], sems.at[i, n])
            for n, src in enumerate(sources)
        ]
        group.append(pltpu.make_async_copy(m_h.at[0].at[rows], mbuf.at[rows], sems.at[i, 6]))
        copies.append(group)
    for copy in copies[0]:
        copy.start()
    for copy in copies[1]:
        copy.start()
    op_copy = pltpu.make_async_copy(op_h.at[0], opbuf, op_sem)
    op_copy.start()

    interval, cos, sin = scene_terms(scene, table)
    col = lax.broadcasted_iota(jnp.int32, (W, 128), 0) // 32
    lane = lax.broadcasted_iota(jnp.int32, (W, 128), 1) % 32
    gather_sum = jnp.where(col == lane, 1.0, 0.0).astype(BF16)
    zeros = jnp.zeros((PAD, W), F32)
    raw_ref[0:PAD, :] = zeros
    raw_ref[PAD + R : WIN, :] = zeros
    prod[0:PAD, :] = zeros[:, :128]
    prod[PAD + rows_all : PAD + rows_all + PAD, :] = zeros[:, :128]

    for i in range(2):
        for copy in copies[i]:
            copy.wait()
        rows = slice(i * half, (i + 1) * half)
        pred = (buf[0, rows] + interval * buf[1, rows]) + (cos * buf[2, rows] - sin * buf[3, rows])
        raw = buf[4, rows] - pred
        raw_ref[PAD + i * half : PAD + (i + 1) * half, :] = raw
        weighted = buf[5, rows] * mbuf[rows].astype(F32) * raw
        high = weighted.astype(BF16)
        low = (weighted - high.astype(F32)).astype(BF16)
        sums[rows] = jnp.dot(high, gather_sum, preferred_element_type=F32) + jnp.dot(
            low, gather_sum, preferred_element_type=F32
        )

    odd = lax.axis_index("tile") % 2 == 1
    first = raw_ref[PAD : PAD + 1, :]
    last = raw_ref[PAD + R - 1 : PAD + R, :]
    ea_ref[...] = jnp.where(odd, first, last)
    eb_ref[...] = jnp.where(odd, last, first)

    block_sums = (sums[...] * BLOCK_SCALE).astype(BF16)
    op_copy.wait()
    step = rows_all // 8
    for i in range(8):
        prod[PAD + i * step : PAD + (i + 1) * step, :] = jnp.dot(
            opbuf[i * step : (i + 1) * step, :], block_sums, preferred_element_type=F32
        )

    quarter = lax.broadcasted_iota(jnp.int32, (SUB, 128), 1) // 32

    def pack(k, carry):
        base = pl.multiple_of(k * R, 8)
        parts = [prod[pl.ds(base + SUB * g, SUB), :] for g in range(4)]
        low_half = jnp.where(quarter == 0, parts[0], parts[1])
        high_half = jnp.where(quarter == 2, parts[2], parts[3])
        part_ref[k] = jnp.where(quarter < 2, low_half, high_half).astype(BF16)
        return carry

    lax.fori_loop(0, tiles, pack, 0, unroll=8)


def front(tiles, scene, table, d, v, s, o, c, m, op):
    rows_all = tiles * R
    return pl.pallas_call(
        functools.partial(front_kernel, tiles),
        out_shape=(
            jax.ShapeDtypeStruct((WIN, W), F32),
            jax.ShapeDtypeStruct((tiles, SUB, 128), BF16),
            jax.ShapeDtypeStruct((1, W), F32),
            jax.ShapeDtypeStruct((1, W), F32),
        ),
        in_specs=[SMEM, SMEM] + [ANY] * 7,
        out_specs=(VMEM,) * 4,
        scratch_shapes=[
            pltpu.VMEM((6, R, W), F32),
            pltpu.VMEM((R, W), jnp.int32),
            pltpu.VMEM((rows_all, R), BF16),
            pltpu.VMEM((R, 128), F32),
            pltpu.VMEM((rows_all + 2 * PAD, 128), F32),
            pltpu.SemaphoreType.DMA((2, 7)),
            pltpu.SemaphoreType.DMA,
        ],
        cost_estimate=pl.CostEstimate(flops=10**8, bytes_accessed=4 * 10**6, transcendentals=0),
        name="front",
    )(scene, table, d, v, s, o, c, m, op)


def cov_kernel(
    scene, table, noise, d_ref, v_ref, s_ref, cd_ref, cc_ref, nv_ref, co_ref, va_ref, cov_ref, xg_ref, we_ref
):
    interval, cos, sin = scene_terms(scene, table)
    rows, cols = 8, 256
    across = W // cols

    def body(n, carry):
        r = pl.ds(pl.multiple_of((n // across) * rows, 8), rows)
        c = pl.ds(pl.multiple_of((n % across) * cols, 128), cols)
        x = [d_ref[0, r, c], v_ref[0, r, c], s_ref[0, 0, r, c], s_ref[1, 0, r, c]]
        diag = [cd_ref[i, 0, r, c] for i in range(4)]
        dev = [jnp.sqrt(e) for e in diag]
        p = [[None] * 4 for _ in range(4)]
        for i in range(4):
            p[i][i] = diag[i]
        for k, (i, j) in enumerate(PAIR_LIST):
            p[i][j] = p[j][i] = cc_ref[k, 0, r, c] * dev[i] * dev[j]
        q = [
            [p[0][j] + interval * p[1][j] for j in range(4)],
            [p[1][j] for j in range(4)],
            [cos * p[2][j] - sin * p[3][j] for j in range(4)],
            [sin * p[2][j] + cos * p[3][j] for j in range(4)],
        ]
        a = [[None] * 4 for _ in range(4)]
        for i in range(4):
            for j in range(i, 4):
                if j == 0:
                    e = q[i][0] + interval * q[i][1]
                elif j == 1:
                    e = q[i][1]
                elif j == 2:
                    e = cos * q[i][2] - sin * q[i][3]
                else:
                    e = sin * q[i][2] + cos * q[i][3]
                if i == j:
                    e = e + noise[i] * interval
                a[i][j] = a[j][i] = e
        pred = [
            x[0] + interval * x[1],
            x[1],
            cos * x[2] - sin * x[3],
            sin * x[2] + cos * x[3],
        ]
        coherence = co_ref[0, r, c]
        valid = va_ref[0, r, c].astype(F32)
        h = [a[i][0] + a[i][2] for i in range(4)]
        variance = h[0] + h[2] + nv_ref[0, r, c] / coherence
        scale = valid / variance
        gain = [h[i] * scale for i in range(4)]
        for i in range(4):
            xg_ref[i, r, c] = pred[i]
            xg_ref[4 + i, r, c] = gain[i]
            cov_ref[i, 0, r, c] = a[i][i] - gain[i] * h[i]
        for k, (i, j) in enumerate(PAIR_LIST):
            cov_ref[4 + k, 0, r, c] = a[i][j] - gain[i] * h[j]
        return carry

    lax.fori_loop(0, (d_ref.shape[1] // rows) * across, body, 0)
    weight = lambda c: co_ref[0, :, c : c + 128] * va_ref[0, :, c : c + 128].astype(F32)
    we_ref[:, :128] = weight(0)
    we_ref[:, 128:] = weight(W - 128)


def covariance(scene, table, noise, d, v, s, cd, cc, nv, co, va):
    step = 16
    plane = pl.BlockSpec((1, step, W), lambda i: (0, i, 0))
    planes = lambda n: pl.BlockSpec((n, 1, step, W), lambda i: (0, 0, i, 0))
    return pl.pallas_call(
        cov_kernel,
        grid=(R // step,),
        out_shape=(
            jax.ShapeDtypeStruct((10, 1, R, W), F32),
            jax.ShapeDtypeStruct((8, R, W), F32),
            jax.ShapeDtypeStruct((R, 256), F32),
        ),
        in_specs=[SMEM] * 3 + [plane, plane, planes(2), planes(4), planes(6), plane, plane, plane],
        out_specs=(
            planes(10),
            pl.BlockSpec((8, step, W), lambda i: (0, i, 0)),
            pl.BlockSpec((step, 256), lambda i: (i, 0)),
        ),
        cost_estimate=pl.CostEstimate(flops=2 * 10**7, bytes_accessed=12 * 10**6, transcendentals=0),
        name="covariance",
    )(scene, table, noise, d, v, s, cd, cc, nv, co, va)


def clean_window(cl, screen, raw_ref, pa_ref, pb_ref, blocks):
    odd = lax.axis_index("tile") % 2 == 1
    lane = lax.broadcasted_iota(jnp.int32, (SUB, 128), 1) // 32
    for g in range(4):
        rows = slice(g * SUB, (g + 1) * SUB)
        for n, b in enumerate(blocks):
            spread = jnp.take_along_axis(screen, lane + (32 * g + 4 * b), axis=1)
            cl[rows, 128 * n : 128 * (n + 1)] = raw_ref[rows, 128 * b : 128 * (b + 1)] - spread
    above = jnp.where(odd, pa_ref[...], pb_ref[...])
    below = jnp.where(odd, pb_ref[...], pa_ref[...])
    for n, b in enumerate(blocks):
        c = slice(128 * n, 128 * (n + 1))
        o = slice(128 * b, 128 * (b + 1))
        cl[PAD - 1 : PAD, c] = cl[PAD - 1 : PAD, c] + above[:, o]
        cl[PAD + R : PAD + R + 1, c] = cl[PAD + R : PAD + R + 1, c] + below[:, o]


def smoothed(up, mid, down):
    width = mid.shape[1]
    col = lax.broadcasted_iota(jnp.int32, mid.shape, 1)
    left = jnp.where(col == 0, 0.0, pltpu.roll(mid, 1, axis=1))
    right = jnp.where(col == width - 1, 0.0, pltpu.roll(mid, width - 1, axis=1))
    return (
        mid
        + ALONG_COEF * (up + down - 2.0 * mid)
        + ACROSS_COEF * (left + right - 2.0 * mid)
    )


def picks(index_row):
    rows = lax.broadcasted_iota(jnp.int32, (R, NB), 0)
    return jnp.where(rows == (index_row >> 3), 1.0, 0.0)


def margin_kernel(
    part_ref, raw_ref, pa_ref, pb_ref, we_ref, up_ref, down_ref, screen_ref, sm_ref, ma_ref, mb_ref, cl
):
    screen = jnp.sum(part_ref[...].astype(F32), axis=0)
    screen_ref[...] = screen
    clean_window(cl, screen, raw_ref, pa_ref, pb_ref, (0, 1, 6, 7))
    smooth = smoothed(cl[PAD - 1 : PAD - 1 + R], cl[PAD : PAD + R], cl[PAD + 1 : PAD + 1 + R])
    sm_ref[:, :128] = smooth[:, :128]
    sm_ref[:, 128:] = smooth[:, 384:]
    odd = lax.axis_index("track") % 2 == 1

    def payload(index_row, weight, value):
        pick = picks(index_row).astype(BF16)
        return [
            lax.dot_general(
                pick, e.astype(BF16), (((0,), (0,)), ((), ())), preferred_element_type=F32
            )
            for e in (weight * value, weight)
        ]

    going_down = payload(down_ref[0], we_ref[:, :128], smooth[:, :128])
    going_up = payload(up_ref[0], we_ref[:, 128:], smooth[:, 384:])
    for n in range(2):
        ma_ref[n] = jnp.where(odd, going_down[n], going_up[n]).astype(BF16)
        mb_ref[n] = jnp.where(odd, going_up[n], going_down[n]).astype(BF16)


def margin(part, raw, pa, pb, we, up, down):
    return pl.pallas_call(
        margin_kernel,
        out_shape=(
            jax.ShapeDtypeStruct((SUB, 128), F32),
            jax.ShapeDtypeStruct((R, 256), F32),
            jax.ShapeDtypeStruct((2, NB, 128), BF16),
            jax.ShapeDtypeStruct((2, NB, 128), BF16),
        ),
        in_specs=[VMEM] * 7,
        out_specs=(VMEM,) * 4,
        scratch_shapes=[pltpu.VMEM((WIN, 512), F32)],
        cost_estimate=pl.CostEstimate(flops=10**7, bytes_accessed=10**6, transcendentals=0),
        name="margin",
    )(part, raw, pa, pb, we, up, down)


def state_kernel(screen_ref, raw_ref, pa_ref, pb_ref, xg_ref, out_ref, cl):
    step = xg_ref.shape[1]

    @pl.when(pl.program_id(0) == 0)
    def _():
        clean_window(cl, screen_ref[...], raw_ref, pa_ref, pb_ref, tuple(range(8)))

    window = cl[pl.ds(pl.multiple_of(pl.program_id(0) * step, 8), step + 2 * PAD), :]
    smooth = smoothed(
        window[PAD - 1 : PAD - 1 + step], window[PAD : PAD + step], window[PAD + 1 : PAD + 1 + step]
    )
    for i in range(4):
        out_ref[i, 0] = xg_ref[i] + xg_ref[4 + i] * smooth


def state(screen, raw, pa, pb, xg):
    step = 16
    whole = lambda shape: pl.BlockSpec(shape, lambda i: (0,) * len(shape))
    return pl.pallas_call(
        state_kernel,
        grid=(R // step,),
        out_shape=jax.ShapeDtypeStruct((4, 1, R, W), F32),
        in_specs=[
            whole((SUB, 128)),
            whole((WIN, W)),
            whole((1, W)),
            whole((1, W)),
            pl.BlockSpec((8, step, W), lambda i: (0, i, 0)),
        ],
        out_specs=pl.BlockSpec((4, 1, step, W), lambda i: (0, 0, i, 0)),
        scratch_shapes=[pltpu.VMEM((WIN, W), F32)],
        cost_estimate=pl.CostEstimate(flops=2 * 10**6, bytes_accessed=4 * 10**6, transcendentals=0),
        name="state",
    )(screen, raw, pa, pb, xg)


def finish_kernel(ra_ref, rb_ref, up_ref, down_ref, sm_ref, we_ref, xg_ref, _, out_ref):
    side = pl.program_id(0)
    odd = lax.axis_index("track") % 2
    use_a = odd != side
    index_row = jnp.where(side == 1, up_ref[0], down_ref[0])
    place = picks(index_row).astype(BF16)
    got = [
        jnp.dot(place, jnp.where(use_a, ra_ref[n].astype(F32), rb_ref[n].astype(F32)).astype(BF16), preferred_element_type=F32)
        for n in range(2)
    ]
    weight = we_ref[...] + WEIGHT_FLOOR
    innovation = (weight * sm_ref[...] + got[0]) / (weight + got[1])
    for i in range(4):
        out_ref[i, 0] = xg_ref[i] + xg_ref[4 + i] * innovation


def finish(ra, rb, up, down, sm, we, xg, ns):
    whole = lambda shape: pl.BlockSpec(shape, lambda i: (0,) * len(shape))
    edge = pl.BlockSpec((R, 128), lambda i: (0, i))
    return pl.pallas_call(
        finish_kernel,
        grid=(2,),
        out_shape=jax.ShapeDtypeStruct(ns.shape, F32),
        in_specs=[
            whole((2, NB, 128)),
            whole((2, NB, 128)),
            whole((1, 1, NB)),
            whole((1, 1, NB)),
            edge,
            edge,
            pl.BlockSpec((8, R, 128), lambda i: (0, 0, 7 * i)),
            ANY,
        ],
        out_specs=pl.BlockSpec((4, 1, R, 128), lambda i: (0, 0, 0, 7 * i)),
        input_output_aliases={7: 0},
        cost_estimate=pl.CostEstimate(flops=10**6, bytes_accessed=10**6, transcendentals=0),
        name="finish",
    )(ra, rb, up, down, sm, we, xg, ns)


def swap(value, axis, first):
    count = lax.axis_size(axis)
    pairs = []
    for i in range(first, count - 1, 2):
        pairs += [(i, i + 1), (i + 1, i)]
    return lax.ppermute(value, axis, pairs)


def local(
    displacement,
    velocity,
    seasonal,
    cov_diag,
    cov_corr,
    observed,
    noise_var,
    coherence,
    valid,
    screen_operator,
    process_noise,
    track_scene,
    scene_interval,
    margin_up,
    margin_down,
):
    tiles = lax.axis_size("tile")
    raw, part, edge_a, edge_b = front(
        tiles, track_scene, scene_interval, displacement, velocity, seasonal, observed, coherence, valid, screen_operator
    )
    part = lax.all_to_all(part, "tile", split_axis=0, concat_axis=0, tiled=True)
    near_a = swap(edge_a, "tile", 0)
    near_b = swap(edge_b, "tile", 1)
    new_cov, xg, edge_weight = covariance(
        track_scene,
        scene_interval,
        process_noise,
        displacement,
        velocity,
        seasonal,
        cov_diag,
        cov_corr,
        noise_var,
        coherence,
        valid,
    )
    screen, edge_smooth, out_a, out_b = margin(
        part, raw, near_a, near_b, edge_weight, margin_up, margin_down
    )
    in_a = swap(out_a, "track", 0)
    in_b = swap(out_b, "track", 1)
    new_state = state(screen, raw, near_a, near_b, xg)
    new_state = finish(in_a, in_b, margin_up, margin_down, edge_smooth, edge_weight, xg, new_state)
    return new_state, new_cov


def solution(mesh):
    in_specs = (
        P("track", "tile", None),
        P("track", "tile", None),
        P(None, "track", "tile", None),
        P(None, "track", "tile", None),
        P(None, "track", "tile", None),
        P("track", "tile", None),
        P("track", "tile", None),
        P("track", "tile", None),
        P("track", "tile", None),
        P("track", None, "tile"),
        P(),
        P("track"),
        P(),
        P("track", "tile", None),
        P("track", "tile", None),
    )
    out_specs = (P(None, "track", "tile", None), P(None, "track", "tile", None))
    return jax.shard_map(local, mesh=mesh, in_specs=in_specs, out_specs=out_specs, check_vma=False)
```

```python
import functools
import math

import jax
import jax.numpy as jnp
from jax import lax
from jax.experimental import pallas as pl
from jax.experimental.pallas import tpu as pltpu
from jax.sharding import PartitionSpec as P

SEASON_RATE = 2.0 * math.pi * 12.0 / 365.25
ALONG_COEF = 0.2
ACROSS_COEF = 0.1
WEIGHT_FLOOR = 0.1
BLOCK_SCALE = 0.25
PAIR_LIST = ((0, 1), (0, 2), (0, 3), (1, 2), (1, 3), (2, 3))

R = 80
W = 1024
PAD = 8
WIN = R + 2 * PAD
SUB = WIN // 4
NB = 40
F32 = jnp.float32
BF16 = jnp.bfloat16

SMEM = pl.BlockSpec(memory_space=pltpu.SMEM)
VMEM = pl.BlockSpec(memory_space=pltpu.VMEM)
ANY = pl.BlockSpec(memory_space=pl.ANY)


def hbm(x):
    return pltpu.with_memory_space_constraint(x, pltpu.HBM)


def vmem(x):
    return pltpu.with_memory_space_constraint(x, pltpu.VMEM)


def scene_terms(scene, table):
    interval = table[scene[0]]
    angle = jnp.full((1, 1), SEASON_RATE * interval, F32)
    return interval, jnp.cos(angle), jnp.sin(angle)


def front_kernel(
    tiles,
    scene_h,
    table_h,
    d_h,
    v_h,
    s_h,
    o_h,
    c_h,
    m_h,
    op_h,
    raw_ref,
    part_ref,
    ea_ref,
    eb_ref,
    terms_ref,
    buf,
    mbuf,
    opbuf,
    sums,
    prod,
    scene,
    table,
    sems,
    op_sem,
    scalar_sems,
):
    scalar_copies = [
        pltpu.make_async_copy(scene_h, scene, scalar_sems.at[0]),
        pltpu.make_async_copy(table_h, table, scalar_sems.at[1]),
    ]
    for copy in scalar_copies:
        copy.start()
    half = R // 2
    rows_all = tiles * R
    copies = []
    for i in range(2):
        rows = pl.ds(i * half, half)
        sources = [d_h.at[0], v_h.at[0], s_h.at[0, 0], s_h.at[1, 0], o_h.at[0], c_h.at[0]]
        group = [
            pltpu.make_async_copy(src.at[rows], buf.at[n, rows], sems.at[i, n])
            for n, src in enumerate(sources)
        ]
        group.append(pltpu.make_async_copy(m_h.at[0].at[rows], mbuf.at[rows], sems.at[i, 6]))
        copies.append(group)
    for copy in copies[0]:
        copy.start()
    for copy in copies[1]:
        copy.start()
    op_copy = pltpu.make_async_copy(op_h.at[0], opbuf, op_sem)
    op_copy.start()

    col = lax.broadcasted_iota(jnp.int32, (W, 128), 0) // 32
    lane = lax.broadcasted_iota(jnp.int32, (W, 128), 1) % 32
    gather_sum = jnp.where(col == lane, 1.0, 0.0).astype(BF16)
    zeros = jnp.zeros((PAD, W), F32)
    raw_ref[0:PAD, :] = zeros
    raw_ref[PAD + R : WIN, :] = zeros
    prod[0:PAD, :] = zeros[:, :128]
    prod[PAD + rows_all : PAD + rows_all + PAD, :] = zeros[:, :128]

    for copy in scalar_copies:
        copy.wait()
    interval, cos, sin = scene_terms(scene, table)
    for n, term in enumerate((interval, cos, sin)):
        terms_ref[n : n + 1, :] = jnp.broadcast_to(term, (1, 128))
    for i in range(2):
        for copy in copies[i]:
            copy.wait()
        rows = slice(i * half, (i + 1) * half)
        pred = (buf[0, rows] + interval * buf[1, rows]) + (cos * buf[2, rows] - sin * buf[3, rows])
        raw = buf[4, rows] - pred
        raw_ref[PAD + i * half : PAD + (i + 1) * half, :] = raw
        weighted = buf[5, rows] * mbuf[rows].astype(F32) * raw
        high = weighted.astype(BF16)
        low = (weighted - high.astype(F32)).astype(BF16)
        sums[rows] = jnp.dot(high, gather_sum, preferred_element_type=F32) + jnp.dot(
            low, gather_sum, preferred_element_type=F32
        )

    odd = lax.axis_index("tile") % 2 == 1
    first = raw_ref[PAD : PAD + 1, :]
    last = raw_ref[PAD + R - 1 : PAD + R, :]
    ea_ref[...] = jnp.where(odd, first, last)
    eb_ref[...] = jnp.where(odd, last, first)

    block_sums = (sums[...] * BLOCK_SCALE).astype(BF16)
    op_copy.wait()
    step = rows_all // 8
    for i in range(8):
        prod[PAD + i * step : PAD + (i + 1) * step, :] = lax.dot_general(
            opbuf[:, i * step : (i + 1) * step],
            block_sums,
            (((0,), (0,)), ((), ())),
            preferred_element_type=F32,
        )

    quarter = lax.broadcasted_iota(jnp.int32, (SUB, 128), 1) // 32

    def pack(k, carry):
        base = pl.multiple_of(k * R, 8)
        parts = [prod[pl.ds(base + SUB * g, SUB), :] for g in range(4)]
        low_half = jnp.where(quarter == 0, parts[0], parts[1])
        high_half = jnp.where(quarter == 2, parts[2], parts[3])
        part_ref[k] = jnp.where(quarter < 2, low_half, high_half).astype(BF16)
        return carry

    lax.fori_loop(0, tiles, pack, 0, unroll=8)


def front(tiles, scene, table, d, v, s, o, c, m, op):
    rows_all = tiles * R
    return pl.pallas_call(
        functools.partial(front_kernel, tiles),
        out_shape=(
            pltpu.VMEM((WIN, W), F32),
            jax.ShapeDtypeStruct((tiles, SUB, 128), BF16),
            jax.ShapeDtypeStruct((1, W), F32),
            jax.ShapeDtypeStruct((1, W), F32),
            pltpu.VMEM((8, 128), F32),
        ),
        in_specs=[ANY] * 9,
        out_specs=(VMEM,) * 5,
        scratch_shapes=[
            pltpu.VMEM((6, R, W), F32),
            pltpu.VMEM((R, W), jnp.int32),
            pltpu.VMEM((R, rows_all), BF16),
            pltpu.VMEM((R, 128), F32),
            pltpu.VMEM((rows_all + 2 * PAD, 128), F32),
            pltpu.SMEM((1,), jnp.int32),
            pltpu.SMEM((16,), F32),
            pltpu.SemaphoreType.DMA((2, 7)),
            pltpu.SemaphoreType.DMA,
            pltpu.SemaphoreType.DMA((2,)),
        ],
        cost_estimate=pl.CostEstimate(flops=10**8, bytes_accessed=4 * 10**6, transcendentals=0),
        compiler_params=pltpu.CompilerParams(vmem_limit_bytes=12 * 2**20),
        name="front",
    )(scene, *map(hbm, (table, d, v, s, o, c, m, op)))


def cov_kernel(
    terms, noise, d_ref, v_ref, s_ref, cd_ref, cc_ref, nv_ref, co_ref, va_ref, cov_ref, xg_ref, we_ref
):
    interval, cos, sin = [terms[n : n + 1, 0:1] for n in range(3)]
    rows, cols = 8, 256
    across = W // cols

    def body(n, carry):
        r = pl.ds(pl.multiple_of((n // across) * rows, 8), rows)
        c = pl.ds(pl.multiple_of((n % across) * cols, 128), cols)
        x = [d_ref[0, r, c], v_ref[0, r, c], s_ref[0, 0, r, c], s_ref[1, 0, r, c]]
        diag = [cd_ref[i, 0, r, c] for i in range(4)]
        dev = [jnp.sqrt(e) for e in diag]
        p = [[None] * 4 for _ in range(4)]
        for i in range(4):
            p[i][i] = diag[i]
        for k, (i, j) in enumerate(PAIR_LIST):
            p[i][j] = p[j][i] = cc_ref[k, 0, r, c] * dev[i] * dev[j]
        q = [
            [p[0][j] + interval * p[1][j] for j in range(4)],
            [p[1][j] for j in range(4)],
            [cos * p[2][j] - sin * p[3][j] for j in range(4)],
            [sin * p[2][j] + cos * p[3][j] for j in range(4)],
        ]
        a = [[None] * 4 for _ in range(4)]
        for i in range(4):
            for j in range(i, 4):
                if j == 0:
                    e = q[i][0] + interval * q[i][1]
                elif j == 1:
                    e = q[i][1]
                elif j == 2:
                    e = cos * q[i][2] - sin * q[i][3]
                else:
                    e = sin * q[i][2] + cos * q[i][3]
                if i == j:
                    e = e + noise[i] * interval
                a[i][j] = a[j][i] = e
        pred = [
            x[0] + interval * x[1],
            x[1],
            cos * x[2] - sin * x[3],
            sin * x[2] + cos * x[3],
        ]
        coherence = co_ref[0, r, c]
        valid = va_ref[0, r, c].astype(F32)
        h = [a[i][0] + a[i][2] for i in range(4)]
        variance = h[0] + h[2] + nv_ref[0, r, c] / coherence
        scale = valid / variance
        gain = [h[i] * scale for i in range(4)]
        for i in range(4):
            xg_ref[i, r, c] = pred[i]
            xg_ref[4 + i, r, c] = gain[i]
            cov_ref[i, 0, r, c] = a[i][i] - gain[i] * h[i]
        for k, (i, j) in enumerate(PAIR_LIST):
            cov_ref[4 + k, 0, r, c] = a[i][j] - gain[i] * h[j]
        return carry

    lax.fori_loop(0, (d_ref.shape[1] // rows) * across, body, 0)
    weight = lambda c: co_ref[0, :, c : c + 128] * va_ref[0, :, c : c + 128].astype(F32)
    we_ref[:, :128] = weight(0)
    we_ref[:, 128:] = weight(W - 128)


def covariance(terms, noise, d, v, s, cd, cc, nv, co, va):
    step = 16
    plane = pl.BlockSpec((1, step, W), lambda i: (0, i, 0))
    planes = lambda n: pl.BlockSpec((n, 1, step, W), lambda i: (0, 0, i, 0))
    return pl.pallas_call(
        cov_kernel,
        grid=(R // step,),
        out_shape=(
            jax.ShapeDtypeStruct((10, 1, R, W), F32),
            pltpu.VMEM((8, R, W), F32),
            pltpu.VMEM((R, 256), F32),
        ),
        in_specs=[pl.BlockSpec((8, 128), lambda i: (0, 0)), SMEM] + [plane, plane, planes(2), planes(4), planes(6), plane, plane, plane],
        out_specs=(
            planes(10),
            pl.BlockSpec((8, step, W), lambda i: (0, i, 0)),
            pl.BlockSpec((step, 256), lambda i: (i, 0)),
        ),
        cost_estimate=pl.CostEstimate(flops=2 * 10**7, bytes_accessed=12 * 10**6, transcendentals=0),
        compiler_params=pltpu.CompilerParams(vmem_limit_bytes=8 * 2**20),
        name="covariance",
    )(vmem(terms), noise, *map(hbm, (d, v, s, cd, cc, nv, co, va)))


def clean_window(cl, screen, raw_ref, pa_ref, pb_ref, blocks):
    odd = lax.axis_index("tile") % 2 == 1
    lane = lax.broadcasted_iota(jnp.int32, (SUB, 128), 1) // 32
    for g in range(4):
        rows = slice(g * SUB, (g + 1) * SUB)
        for n, b in enumerate(blocks):
            spread = jnp.take_along_axis(screen, lane + (32 * g + 4 * b), axis=1)
            cl[rows, 128 * n : 128 * (n + 1)] = raw_ref[rows, 128 * b : 128 * (b + 1)] - spread
    above = jnp.where(odd, pa_ref[...], pb_ref[...])
    below = jnp.where(odd, pb_ref[...], pa_ref[...])
    for n, b in enumerate(blocks):
        c = slice(128 * n, 128 * (n + 1))
        o = slice(128 * b, 128 * (b + 1))
        cl[PAD - 1 : PAD, c] = cl[PAD - 1 : PAD, c] + above[:, o]
        cl[PAD + R : PAD + R + 1, c] = cl[PAD + R : PAD + R + 1, c] + below[:, o]


def smoothed(up, mid, down):
    width = mid.shape[1]
    col = lax.broadcasted_iota(jnp.int32, mid.shape, 1)
    left = jnp.where(col == 0, 0.0, pltpu.roll(mid, 1, axis=1))
    right = jnp.where(col == width - 1, 0.0, pltpu.roll(mid, width - 1, axis=1))
    return (
        mid
        + ALONG_COEF * (up + down - 2.0 * mid)
        + ACROSS_COEF * (left + right - 2.0 * mid)
    )


def picks(index_row):
    rows = lax.broadcasted_iota(jnp.int32, (R, NB), 0)
    return jnp.where(rows == (index_row >> 3), 1.0, 0.0)


def margin_kernel(
    part_ref, raw_ref, pa_ref, pb_ref, we_ref, up_ref, down_ref, screen_ref, sm_ref, ma_ref, mb_ref, cl
):
    screen = jnp.sum(part_ref[...].astype(F32), axis=0)
    screen_ref[...] = screen
    clean_window(cl, screen, raw_ref, pa_ref, pb_ref, (0, 1, 6, 7))
    smooth = smoothed(cl[PAD - 1 : PAD - 1 + R], cl[PAD : PAD + R], cl[PAD + 1 : PAD + 1 + R])
    sm_ref[:, :128] = smooth[:, :128]
    sm_ref[:, 128:] = smooth[:, 384:]
    odd = lax.axis_index("track") % 2 == 1

    def payload(index_row, weight, value):
        pick = picks(index_row).astype(BF16)
        return [
            lax.dot_general(
                pick, e.astype(BF16), (((0,), (0,)), ((), ())), preferred_element_type=F32
            )
            for e in (weight * value, weight)
        ]

    going_down = payload(down_ref[0], we_ref[:, :128], smooth[:, :128])
    going_up = payload(up_ref[0], we_ref[:, 128:], smooth[:, 384:])
    for n in range(2):
        ma_ref[n] = jnp.where(odd, going_down[n], going_up[n]).astype(BF16)
        mb_ref[n] = jnp.where(odd, going_up[n], going_down[n]).astype(BF16)


def margin(part, raw, pa, pb, we, up, down):
    return pl.pallas_call(
        margin_kernel,
        out_shape=(
            pltpu.VMEM((SUB, 128), F32),
            pltpu.VMEM((R, 256), F32),
            jax.ShapeDtypeStruct((2, NB, 128), BF16),
            jax.ShapeDtypeStruct((2, NB, 128), BF16),
        ),
        in_specs=[VMEM] * 7,
        out_specs=(VMEM,) * 4,
        scratch_shapes=[pltpu.VMEM((WIN, 512), F32)],
        cost_estimate=pl.CostEstimate(flops=10**7, bytes_accessed=10**6, transcendentals=0),
        compiler_params=pltpu.CompilerParams(vmem_limit_bytes=2 * 2**20),
        name="margin",
    )(part, vmem(raw), pa, pb, vmem(we), up, down)


def state_kernel(screen_ref, raw_ref, pa_ref, pb_ref, xg_ref, out_ref, cl):
    step = xg_ref.shape[1]

    @pl.when(pl.program_id(0) == 0)
    def _():
        clean_window(cl, screen_ref[...], raw_ref, pa_ref, pb_ref, tuple(range(8)))

    window = cl[pl.ds(pl.multiple_of(pl.program_id(0) * step, 8), step + 2 * PAD), :]
    smooth = smoothed(
        window[PAD - 1 : PAD - 1 + step], window[PAD : PAD + step], window[PAD + 1 : PAD + 1 + step]
    )
    for i in range(4):
        out_ref[i, 0] = xg_ref[i] + xg_ref[4 + i] * smooth


def state(screen, raw, pa, pb, xg):
    step = 16
    whole = lambda shape: pl.BlockSpec(shape, lambda i: (0,) * len(shape))
    return pl.pallas_call(
        state_kernel,
        grid=(R // step,),
        out_shape=pltpu.HBM((4, 1, R, W), F32),
        in_specs=[
            whole((SUB, 128)),
            whole((WIN, W)),
            whole((1, W)),
            whole((1, W)),
            pl.BlockSpec((8, step, W), lambda i: (0, i, 0)),
        ],
        out_specs=pl.BlockSpec((4, 1, step, W), lambda i: (0, 0, i, 0)),
        scratch_shapes=[pltpu.VMEM((WIN, W), F32)],
        cost_estimate=pl.CostEstimate(flops=2 * 10**6, bytes_accessed=4 * 10**6, transcendentals=0),
        compiler_params=pltpu.CompilerParams(vmem_limit_bytes=6 * 2**20),
        name="state",
    )(vmem(screen), vmem(raw), pa, pb, vmem(xg))


def finish_kernel(ra_ref, rb_ref, up_ref, down_ref, sm_ref, we_ref, xg_ref, _, out_ref):
    side = pl.program_id(0)
    odd = lax.axis_index("track") % 2
    use_a = odd != side
    index_row = jnp.where(side == 1, up_ref[0], down_ref[0])
    place = picks(index_row).astype(BF16)
    got = [
        jnp.dot(place, jnp.where(use_a, ra_ref[n].astype(F32), rb_ref[n].astype(F32)).astype(BF16), preferred_element_type=F32)
        for n in range(2)
    ]
    weight = we_ref[...] + WEIGHT_FLOOR
    innovation = (weight * sm_ref[...] + got[0]) / (weight + got[1])
    for i in range(4):
        out_ref[i, 0] = xg_ref[i] + xg_ref[4 + i] * innovation


def finish(ra, rb, up, down, sm, we, xg, ns):
    whole = lambda shape: pl.BlockSpec(shape, lambda i: (0,) * len(shape))
    edge = pl.BlockSpec((R, 128), lambda i: (0, i))
    return pl.pallas_call(
        finish_kernel,
        grid=(2,),
        out_shape=jax.ShapeDtypeStruct(ns.shape, F32),
        in_specs=[
            whole((2, NB, 128)),
            whole((2, NB, 128)),
            whole((1, 1, NB)),
            whole((1, 1, NB)),
            edge,
            edge,
            pl.BlockSpec((8, R, 128), lambda i: (0, 0, 7 * i)),
            ANY,
        ],
        out_specs=pl.BlockSpec((4, 1, R, 128), lambda i: (0, 0, 0, 7 * i)),
        input_output_aliases={7: 0},
        cost_estimate=pl.CostEstimate(flops=10**6, bytes_accessed=10**6, transcendentals=0),
        compiler_params=pltpu.CompilerParams(vmem_limit_bytes=3 * 2**20),
        name="finish",
    )(ra, rb, up, down, vmem(sm), vmem(we), vmem(xg), ns)


def swap(value, axis, first):
    count = lax.axis_size(axis)
    pairs = []
    for i in range(first, count - 1, 2):
        pairs += [(i, i + 1), (i + 1, i)]
    return lax.ppermute(value, axis, pairs)


def local(
    displacement,
    velocity,
    seasonal,
    cov_diag,
    cov_corr,
    observed,
    noise_var,
    coherence,
    valid,
    screen_operator,
    process_noise,
    track_scene,
    scene_interval,
    margin_up,
    margin_down,
):
    tiles = lax.axis_size("tile")
    raw, part, edge_a, edge_b, terms = front(
        tiles, track_scene, scene_interval, displacement, velocity, seasonal, observed, coherence, valid, jnp.swapaxes(screen_operator, 1, 2)
    )
    part = lax.all_to_all(part, "tile", split_axis=0, concat_axis=0, tiled=True)
    near_a = swap(edge_a, "tile", 0)
    near_b = swap(edge_b, "tile", 1)
    new_cov, xg, edge_weight = covariance(
        terms,
        process_noise,
        displacement,
        velocity,
        seasonal,
        cov_diag,
        cov_corr,
        noise_var,
        coherence,
        valid,
    )
    screen, edge_smooth, out_a, out_b = margin(
        part, raw, near_a, near_b, edge_weight, margin_up, margin_down
    )
    in_a = swap(out_a, "track", 0)
    in_b = swap(out_b, "track", 1)
    new_state = state(screen, raw, near_a, near_b, xg)
    new_state = finish(in_a, in_b, margin_up, margin_down, edge_smooth, edge_weight, xg, new_state)
    return new_state, new_cov


def solution(mesh):
    in_specs = (
        P("track", "tile", None),
        P("track", "tile", None),
        P(None, "track", "tile", None),
        P(None, "track", "tile", None),
        P(None, "track", "tile", None),
        P("track", "tile", None),
        P("track", "tile", None),
        P("track", "tile", None),
        P("track", "tile", None),
        P("track", None, "tile"),
        P(),
        P("track"),
        P(),
        P("track", "tile", None),
        P("track", "tile", None),
    )
    out_specs = (P(None, "track", "tile", None), P(None, "track", "tile", None))
    return jax.shard_map(local, mesh=mesh, in_specs=in_specs, out_specs=out_specs, check_vma=False)
```

```python
import functools
import math

import jax
import jax.numpy as jnp
from jax import lax
from jax.experimental import pallas as pl
from jax.experimental.pallas import tpu as pltpu
from jax.sharding import PartitionSpec as P

SEASON_RATE = 2.0 * math.pi * 12.0 / 365.25
ALONG_COEF = 0.2
ACROSS_COEF = 0.1
WEIGHT_FLOOR = 0.1
BLOCK_SCALE = 0.25
PAIR_LIST = ((0, 1), (0, 2), (0, 3), (1, 2), (1, 3), (2, 3))

R = 80
W = 1024
PAD = 8
WIN = R + 2 * PAD
SUB = WIN // 4
NB = 40
F32 = jnp.float32
BF16 = jnp.bfloat16

SMEM = pl.BlockSpec(memory_space=pltpu.SMEM)
VMEM = pl.BlockSpec(memory_space=pltpu.VMEM)
ANY = pl.BlockSpec(memory_space=pl.ANY)


def hbm(x):
    return pltpu.with_memory_space_constraint(x, pltpu.HBM)


def vmem(x):
    return pltpu.with_memory_space_constraint(x, pltpu.VMEM)


def scene_terms(scene, table):
    interval = table[scene[0]]
    angle = jnp.full((1, 1), SEASON_RATE * interval, F32)
    return interval, jnp.cos(angle), jnp.sin(angle)


def front_kernel(
    tiles,
    scene_h,
    table_h,
    d_h,
    v_h,
    s_h,
    o_h,
    c_h,
    m_h,
    op_h,
    raw_ref,
    part_ref,
    ea_ref,
    eb_ref,
    terms_ref,
    buf,
    mbuf,
    opbuf,
    sums,
    prod,
    scene,
    table,
    sems,
    op_sem,
    scalar_sems,
):
    scalar_copies = [
        pltpu.make_async_copy(scene_h, scene, scalar_sems.at[0]),
        pltpu.make_async_copy(table_h, table, scalar_sems.at[1]),
    ]
    for copy in scalar_copies:
        copy.start()
    half = R // 2
    rows_all = tiles * R
    copies = []
    for i in range(2):
        rows = pl.ds(i * half, half)
        sources = [d_h.at[0], v_h.at[0], s_h.at[0, 0], s_h.at[1, 0], o_h.at[0], c_h.at[0]]
        group = [
            pltpu.make_async_copy(src.at[rows], buf.at[n, rows], sems.at[i, n])
            for n, src in enumerate(sources)
        ]
        group.append(pltpu.make_async_copy(m_h.at[0].at[rows], mbuf.at[rows], sems.at[i, 6]))
        copies.append(group)
    for copy in copies[0]:
        copy.start()
    for copy in copies[1]:
        copy.start()
    op_copy = pltpu.make_async_copy(op_h.at[0], opbuf, op_sem)
    op_copy.start()

    col = lax.broadcasted_iota(jnp.int32, (W, 128), 0) // 32
    lane = lax.broadcasted_iota(jnp.int32, (W, 128), 1) % 32
    gather_sum = jnp.where(col == lane, 1.0, 0.0).astype(BF16)
    zeros = jnp.zeros((PAD, W), F32)
    raw_ref[0:PAD, :] = zeros
    raw_ref[PAD + R : WIN, :] = zeros
    prod[0:PAD, :] = zeros[:, :128]
    prod[PAD + rows_all : PAD + rows_all + PAD, :] = zeros[:, :128]

    for copy in scalar_copies:
        copy.wait()
    interval, cos, sin = scene_terms(scene, table)
    for n, term in enumerate((interval, cos, sin)):
        terms_ref[n : n + 1, :] = jnp.broadcast_to(term, (1, 128))
    for i in range(2):
        for copy in copies[i]:
            copy.wait()
        rows = slice(i * half, (i + 1) * half)
        pred = (buf[0, rows] + interval * buf[1, rows]) + (cos * buf[2, rows] - sin * buf[3, rows])
        raw = buf[4, rows] - pred
        raw_ref[PAD + i * half : PAD + (i + 1) * half, :] = raw
        weighted = buf[5, rows] * mbuf[rows].astype(F32) * raw
        high = weighted.astype(BF16)
        low = (weighted - high.astype(F32)).astype(BF16)
        sums[rows] = jnp.dot(high, gather_sum, preferred_element_type=F32) + jnp.dot(
            low, gather_sum, preferred_element_type=F32
        )

    tile = lax.axis_index("tile")
    odd = tile % 2 == 1
    first = raw_ref[PAD : PAD + 1, :]
    last = raw_ref[PAD + R - 1 : PAD + R, :]
    ea_ref[...] = jnp.where(odd, first, last)
    at_end = (tile == 0) | (tile == tiles - 1)
    eb_ref[...] = jnp.where(at_end, 0.0, jnp.where(odd, last, first))

    block_sums = (sums[...] * BLOCK_SCALE).astype(BF16)
    op_copy.wait()
    step = rows_all // 8
    for i in range(8):
        prod[PAD + i * step : PAD + (i + 1) * step, :] = lax.dot_general(
            opbuf[:, i * step : (i + 1) * step],
            block_sums,
            (((0,), (0,)), ((), ())),
            preferred_element_type=F32,
        )

    quarter = lax.broadcasted_iota(jnp.int32, (SUB, 128), 1) // 32

    def pack(k, carry):
        base = pl.multiple_of(k * R, 8)
        parts = [prod[pl.ds(base + SUB * g, SUB), :] for g in range(4)]
        low_half = jnp.where(quarter == 0, parts[0], parts[1])
        high_half = jnp.where(quarter == 2, parts[2], parts[3])
        part_ref[k] = jnp.where(quarter < 2, low_half, high_half).astype(BF16)
        return carry

    lax.fori_loop(0, tiles, pack, 0, unroll=8)


def front(tiles, scene, table, d, v, s, o, c, m, op):
    rows_all = tiles * R
    return pl.pallas_call(
        functools.partial(front_kernel, tiles),
        out_shape=(
            pltpu.VMEM((WIN, W), F32),
            jax.ShapeDtypeStruct((tiles, SUB, 128), BF16),
            jax.ShapeDtypeStruct((1, W), F32),
            jax.ShapeDtypeStruct((1, W), F32),
            pltpu.VMEM((8, 128), F32),
        ),
        in_specs=[ANY] * 9,
        out_specs=(VMEM,) * 5,
        scratch_shapes=[
            pltpu.VMEM((6, R, W), F32),
            pltpu.VMEM((R, W), jnp.int32),
            pltpu.VMEM((R, rows_all), BF16),
            pltpu.VMEM((R, 128), F32),
            pltpu.VMEM((rows_all + 2 * PAD, 128), F32),
            pltpu.SMEM((1,), jnp.int32),
            pltpu.SMEM((16,), F32),
            pltpu.SemaphoreType.DMA((2, 7)),
            pltpu.SemaphoreType.DMA,
            pltpu.SemaphoreType.DMA((2,)),
        ],
        cost_estimate=pl.CostEstimate(flops=10**8, bytes_accessed=4 * 10**6, transcendentals=0),
        compiler_params=pltpu.CompilerParams(vmem_limit_bytes=12 * 2**20),
        name="front",
    )(scene, *map(hbm, (table, d, v, s, o, c, m, op)))


def cov_kernel(
    terms, noise, d_ref, v_ref, s_ref, cd_ref, cc_ref, nv_ref, co_ref, va_ref, cov_ref, xg_ref, we_ref
):
    interval, cos, sin = [terms[n : n + 1, 0:1] for n in range(3)]
    rows, cols = 8, 256
    across = W // cols

    def body(n, carry):
        r = pl.ds(pl.multiple_of((n // across) * rows, 8), rows)
        c = pl.ds(pl.multiple_of((n % across) * cols, 128), cols)
        x = [d_ref[0, r, c], v_ref[0, r, c], s_ref[0, 0, r, c], s_ref[1, 0, r, c]]
        diag = [cd_ref[i, 0, r, c] for i in range(4)]
        dev = [jnp.sqrt(e) for e in diag]
        p = [[None] * 4 for _ in range(4)]
        for i in range(4):
            p[i][i] = diag[i]
        for k, (i, j) in enumerate(PAIR_LIST):
            p[i][j] = p[j][i] = cc_ref[k, 0, r, c] * dev[i] * dev[j]
        q = [
            [p[0][j] + interval * p[1][j] for j in range(4)],
            [p[1][j] for j in range(4)],
            [cos * p[2][j] - sin * p[3][j] for j in range(4)],
            [sin * p[2][j] + cos * p[3][j] for j in range(4)],
        ]
        a = [[None] * 4 for _ in range(4)]
        for i in range(4):
            for j in range(i, 4):
                if j == 0:
                    e = q[i][0] + interval * q[i][1]
                elif j == 1:
                    e = q[i][1]
                elif j == 2:
                    e = cos * q[i][2] - sin * q[i][3]
                else:
                    e = sin * q[i][2] + cos * q[i][3]
                if i == j:
                    e = e + noise[i] * interval
                a[i][j] = a[j][i] = e
        pred = [
            x[0] + interval * x[1],
            x[1],
            cos * x[2] - sin * x[3],
            sin * x[2] + cos * x[3],
        ]
        coherence = co_ref[0, r, c]
        valid = va_ref[0, r, c].astype(F32)
        h = [a[i][0] + a[i][2] for i in range(4)]
        variance = h[0] + h[2] + nv_ref[0, r, c] / coherence
        scale = valid / variance
        gain = [h[i] * scale for i in range(4)]
        for i in range(4):
            xg_ref[i, r, c] = pred[i]
            xg_ref[4 + i, r, c] = gain[i]
            cov_ref[i, 0, r, c] = a[i][i] - gain[i] * h[i]
        for k, (i, j) in enumerate(PAIR_LIST):
            cov_ref[4 + k, 0, r, c] = a[i][j] - gain[i] * h[j]
        return carry

    lax.fori_loop(0, (d_ref.shape[1] // rows) * across, body, 0)
    weight = lambda c: co_ref[0, :, c : c + 128] * va_ref[0, :, c : c + 128].astype(F32)
    we_ref[:, :128] = weight(0)
    we_ref[:, 128:] = weight(W - 128)


def covariance(terms, noise, d, v, s, cd, cc, nv, co, va):
    step = 16
    plane = pl.BlockSpec((1, step, W), lambda i: (0, i, 0))
    planes = lambda n: pl.BlockSpec((n, 1, step, W), lambda i: (0, 0, i, 0))
    return pl.pallas_call(
        cov_kernel,
        grid=(R // step,),
        out_shape=(
            jax.ShapeDtypeStruct((10, 1, R, W), F32),
            pltpu.VMEM((8, R, W), F32),
            pltpu.VMEM((R, 256), F32),
        ),
        in_specs=[pl.BlockSpec((8, 128), lambda i: (0, 0)), SMEM] + [plane, plane, planes(2), planes(4), planes(6), plane, plane, plane],
        out_specs=(
            planes(10),
            pl.BlockSpec((8, step, W), lambda i: (0, i, 0)),
            pl.BlockSpec((step, 256), lambda i: (i, 0)),
        ),
        cost_estimate=pl.CostEstimate(flops=2 * 10**7, bytes_accessed=12 * 10**6, transcendentals=0),
        compiler_params=pltpu.CompilerParams(vmem_limit_bytes=8 * 2**20),
        name="covariance",
    )(vmem(terms), noise, *map(hbm, (d, v, s, cd, cc, nv, co, va)))


def clean_window(cl, screen, raw_ref, pa_ref, pb_ref, blocks):
    odd = lax.axis_index("tile") % 2 == 1
    lane = lax.broadcasted_iota(jnp.int32, (SUB, 128), 1) // 32
    for g in range(4):
        rows = slice(g * SUB, (g + 1) * SUB)
        for n, b in enumerate(blocks):
            spread = jnp.take_along_axis(screen, lane + (32 * g + 4 * b), axis=1)
            cl[rows, 128 * n : 128 * (n + 1)] = raw_ref[rows, 128 * b : 128 * (b + 1)] - spread
    above = jnp.where(odd, pa_ref[...], pb_ref[...])
    below = jnp.where(odd, pb_ref[...], pa_ref[...])
    for n, b in enumerate(blocks):
        c = slice(128 * n, 128 * (n + 1))
        o = slice(128 * b, 128 * (b + 1))
        cl[PAD - 1 : PAD, c] = cl[PAD - 1 : PAD, c] + above[:, o]
        cl[PAD + R : PAD + R + 1, c] = cl[PAD + R : PAD + R + 1, c] + below[:, o]


def smoothed(up, mid, down):
    width = mid.shape[1]
    col = lax.broadcasted_iota(jnp.int32, mid.shape, 1)
    left = jnp.where(col == 0, 0.0, pltpu.roll(mid, 1, axis=1))
    right = jnp.where(col == width - 1, 0.0, pltpu.roll(mid, width - 1, axis=1))
    return (
        mid
        + ALONG_COEF * (up + down - 2.0 * mid)
        + ACROSS_COEF * (left + right - 2.0 * mid)
    )


def picks(index_row):
    rows = lax.broadcasted_iota(jnp.int32, (R, NB), 0)
    return jnp.where(rows == (index_row >> 3), 1.0, 0.0)


def margin_kernel(
    part_ref, raw_ref, pa_ref, pb_ref, we_ref, up_ref, down_ref, screen_ref, sm_ref, ma_ref, mb_ref, cl
):
    screen = jnp.sum(part_ref[...].astype(F32), axis=0)
    screen_ref[...] = screen
    clean_window(cl, screen, raw_ref, pa_ref, pb_ref, (0, 1, 6, 7))
    smooth = smoothed(cl[PAD - 1 : PAD - 1 + R], cl[PAD : PAD + R], cl[PAD + 1 : PAD + 1 + R])
    sm_ref[:, :128] = smooth[:, :128]
    sm_ref[:, 128:] = smooth[:, 384:]
    odd = lax.axis_index("track") % 2 == 1

    def payload(index_row, weight, value):
        pick = picks(index_row).astype(BF16)
        return [
            lax.dot_general(
                pick, e.astype(BF16), (((0,), (0,)), ((), ())), preferred_element_type=F32
            )
            for e in (weight * value, weight)
        ]

    going_down = payload(down_ref[0], we_ref[:, :128], smooth[:, :128])
    going_up = payload(up_ref[0], we_ref[:, 128:], smooth[:, 384:])
    for n in range(2):
        ma_ref[n] = jnp.where(odd, going_down[n], going_up[n]).astype(BF16)
        mb_ref[n] = jnp.where(odd, going_up[n], going_down[n]).astype(BF16)


def margin(part, raw, pa, pb, we, up, down):
    return pl.pallas_call(
        margin_kernel,
        out_shape=(
            pltpu.VMEM((SUB, 128), F32),
            pltpu.VMEM((R, 256), F32),
            jax.ShapeDtypeStruct((2, NB, 128), BF16),
            jax.ShapeDtypeStruct((2, NB, 128), BF16),
        ),
        in_specs=[VMEM] * 7,
        out_specs=(VMEM,) * 4,
        scratch_shapes=[pltpu.VMEM((WIN, 512), F32)],
        cost_estimate=pl.CostEstimate(flops=10**7, bytes_accessed=10**6, transcendentals=0),
        compiler_params=pltpu.CompilerParams(vmem_limit_bytes=2 * 2**20),
        name="margin",
    )(part, vmem(raw), pa, pb, vmem(we), up, down)


def state_kernel(screen_ref, raw_ref, pa_ref, pb_ref, xg_ref, out_ref, cl):
    step = xg_ref.shape[1]

    @pl.when(pl.program_id(0) == 0)
    def _():
        clean_window(cl, screen_ref[...], raw_ref, pa_ref, pb_ref, tuple(range(8)))

    window = cl[pl.ds(pl.multiple_of(pl.program_id(0) * step, 8), step + 2 * PAD), :]
    smooth = smoothed(
        window[PAD - 1 : PAD - 1 + step], window[PAD : PAD + step], window[PAD + 1 : PAD + 1 + step]
    )
    for i in range(4):
        out_ref[i, 0] = xg_ref[i] + xg_ref[4 + i] * smooth


def state(screen, raw, pa, pb, xg):
    step = 16
    whole = lambda shape: pl.BlockSpec(shape, lambda i: (0,) * len(shape))
    return pl.pallas_call(
        state_kernel,
        grid=(R // step,),
        out_shape=pltpu.HBM((4, 1, R, W), F32),
        in_specs=[
            whole((SUB, 128)),
            whole((WIN, W)),
            whole((1, W)),
            whole((1, W)),
            pl.BlockSpec((8, step, W), lambda i: (0, i, 0)),
        ],
        out_specs=pl.BlockSpec((4, 1, step, W), lambda i: (0, 0, i, 0)),
        scratch_shapes=[pltpu.VMEM((WIN, W), F32)],
        cost_estimate=pl.CostEstimate(flops=2 * 10**6, bytes_accessed=4 * 10**6, transcendentals=0),
        compiler_params=pltpu.CompilerParams(vmem_limit_bytes=6 * 2**20),
        name="state",
    )(vmem(screen), vmem(raw), pa, pb, vmem(xg))


def finish_kernel(ra_ref, rb_ref, up_ref, down_ref, sm_ref, we_ref, xg_ref, _, out_ref):
    side = pl.program_id(0)
    odd = lax.axis_index("track") % 2
    use_a = odd != side
    index_row = jnp.where(side == 1, up_ref[0], down_ref[0])
    place = picks(index_row).astype(BF16)
    got = [
        jnp.dot(place, jnp.where(use_a, ra_ref[n].astype(F32), rb_ref[n].astype(F32)).astype(BF16), preferred_element_type=F32)
        for n in range(2)
    ]
    weight = we_ref[...] + WEIGHT_FLOOR
    innovation = (weight * sm_ref[...] + got[0]) / (weight + got[1])
    for i in range(4):
        out_ref[i, 0] = xg_ref[i] + xg_ref[4 + i] * innovation


def finish(ra, rb, up, down, sm, we, xg, ns):
    whole = lambda shape: pl.BlockSpec(shape, lambda i: (0,) * len(shape))
    edge = pl.BlockSpec((R, 128), lambda i: (0, i))
    return pl.pallas_call(
        finish_kernel,
        grid=(2,),
        out_shape=jax.ShapeDtypeStruct(ns.shape, F32),
        in_specs=[
            whole((2, NB, 128)),
            whole((2, NB, 128)),
            whole((1, 1, NB)),
            whole((1, 1, NB)),
            edge,
            edge,
            pl.BlockSpec((8, R, 128), lambda i: (0, 0, 7 * i)),
            ANY,
        ],
        out_specs=pl.BlockSpec((4, 1, R, 128), lambda i: (0, 0, 0, 7 * i)),
        input_output_aliases={7: 0},
        cost_estimate=pl.CostEstimate(flops=10**6, bytes_accessed=10**6, transcendentals=0),
        compiler_params=pltpu.CompilerParams(vmem_limit_bytes=3 * 2**20),
        name="finish",
    )(ra, rb, up, down, vmem(sm), vmem(we), vmem(xg), ns)


def swap(value, axis, first):
    count = lax.axis_size(axis)
    pairs = []
    for i in range(first, first + count, 2):
        a, b = i % count, (i + 1) % count
        pairs += [(a, b), (b, a)]
    return lax.ppermute(value, axis, pairs)


def local(
    displacement,
    velocity,
    seasonal,
    cov_diag,
    cov_corr,
    observed,
    noise_var,
    coherence,
    valid,
    screen_operator,
    process_noise,
    track_scene,
    scene_interval,
    margin_up,
    margin_down,
):
    tiles = lax.axis_size("tile")
    raw, part, edge_a, edge_b, terms = front(
        tiles, track_scene, scene_interval, displacement, velocity, seasonal, observed, coherence, valid, jnp.swapaxes(screen_operator, 1, 2)
    )
    part = lax.all_to_all(part, "tile", split_axis=0, concat_axis=0, tiled=True)
    near_a = swap(edge_a, "tile", 0)
    near_b = swap(edge_b, "tile", 1)
    new_cov, xg, edge_weight = covariance(
        terms,
        process_noise,
        displacement,
        velocity,
        seasonal,
        cov_diag,
        cov_corr,
        noise_var,
        coherence,
        valid,
    )
    screen, edge_smooth, out_a, out_b = margin(
        part, raw, near_a, near_b, edge_weight, margin_up, margin_down
    )
    in_b = swap(out_b, "track", 1)
    in_a = swap(out_a, "track", 0)
    new_state = state(screen, raw, near_a, near_b, xg)
    new_state = finish(in_a, in_b, margin_up, margin_down, edge_smooth, edge_weight, xg, new_state)
    return new_state, new_cov


def solution(mesh):
    in_specs = (
        P("track", "tile", None),
        P("track", "tile", None),
        P(None, "track", "tile", None),
        P(None, "track", "tile", None),
        P(None, "track", "tile", None),
        P("track", "tile", None),
        P("track", "tile", None),
        P("track", "tile", None),
        P("track", "tile", None),
        P("track", None, "tile"),
        P(),
        P("track"),
        P(),
        P("track", "tile", None),
        P("track", "tile", None),
    )
    out_specs = (P(None, "track", "tile", None), P(None, "track", "tile", None))
    return jax.shard_map(local, mesh=mesh, in_specs=in_specs, out_specs=out_specs, check_vma=False)
```

```python
import functools
import math

import jax
import jax.numpy as jnp
from jax import lax
from jax.experimental import pallas as pl
from jax.experimental.pallas import tpu as pltpu
from jax.sharding import PartitionSpec as P


SEASON_RATE = 2.0 * math.pi * 12.0 / 365.25
ALONG_COEF = 0.2
ACROSS_COEF = 0.1
WEIGHT_FLOOR = 0.1
BLOCK_SCALE = 0.25
PAIR_LIST = ((0, 1), (0, 2), (0, 3), (1, 2), (1, 3), (2, 3))

R = 80
W = 1024
PAD = 8
WIN = R + 2 * PAD
SUB = WIN // 4
NB = 40
SHARE = 16
F32 = jnp.float32
BF16 = jnp.bfloat16

SMEM = pl.BlockSpec(memory_space=pltpu.SMEM)
VMEM = pl.BlockSpec(memory_space=pltpu.VMEM)
ANY = pl.BlockSpec(memory_space=pl.ANY)


def hbm(x):
    return pltpu.with_memory_space_constraint(x, pltpu.HBM)


def vmem(x):
    return pltpu.with_memory_space_constraint(x, pltpu.VMEM)


def scene_terms(scene, table):
    interval = table[scene[0]]
    angle = jnp.full((1, 1), SEASON_RATE * interval, F32)
    return interval, jnp.cos(angle), jnp.sin(angle)


def front_kernel(
    tiles,
    scene_h,
    table_h,
    d_h,
    v_h,
    s_h,
    o_h,
    c_h,
    m_h,
    op_h,
    raw_ref,
    part_ref,
    ea_ref,
    eb_ref,
    terms_ref,
    buf,
    mbuf,
    opbuf,
    split,
    prod,
    packed,
    scene,
    table,
    sems,
    op_sem,
    scalar_sems,
    out_sems,
):
    scalar_copies = [
        pltpu.make_async_copy(scene_h, scene, scalar_sems.at[0]),
        pltpu.make_async_copy(table_h, table, scalar_sems.at[1]),
    ]
    for copy in scalar_copies:
        copy.start()
    cuts = ((0, 48), (48, 32))
    rows_all = tiles * R
    copies = []
    for i in range(2):
        rows = pl.ds(*cuts[i])
        sources = [d_h.at[0], v_h.at[0], s_h.at[0, 0], s_h.at[1, 0], o_h.at[0], c_h.at[0]]
        group = [
            pltpu.make_async_copy(src.at[rows], buf.at[n, rows], sems.at[i, n])
            for n, src in enumerate(sources)
        ]
        group.append(pltpu.make_async_copy(m_h.at[0].at[rows], mbuf.at[rows], sems.at[i, 6]))
        copies.append(group)
    for copy in copies[0]:
        copy.start()
    for copy in copies[1]:
        copy.start()
    op_copy = pltpu.make_async_copy(op_h.at[0], opbuf, op_sem)
    op_copy.start()

    col = lax.broadcasted_iota(jnp.int32, (W, 128), 0) // 32
    lane = lax.broadcasted_iota(jnp.int32, (W, 128), 1) % 32
    gather_sum = jnp.where(col == lane, 1.0, 0.0).astype(BF16)
    zeros = jnp.zeros((PAD, W), F32)
    raw_ref[0:PAD, :] = zeros
    raw_ref[PAD + R : WIN, :] = zeros
    prod[0:PAD, :] = zeros[:, :128]
    prod[PAD + rows_all : PAD + rows_all + PAD, :] = zeros[:, :128]

    for copy in scalar_copies:
        copy.wait()
    interval, cos, sin = scene_terms(scene, table)
    for n, term in enumerate((interval, cos, sin)):
        terms_ref[n : n + 1, :] = jnp.broadcast_to(term, (1, 128))
    for i in range(2):
        for copy in copies[i]:
            copy.wait()
        at, size = cuts[i]
        for r0 in range(at, at + size, 16):
            for c0 in range(0, W, 256):
                r, c = slice(r0, r0 + 16), slice(c0, c0 + 256)
                pred = (buf[0, r, c] + interval * buf[1, r, c]) + (
                    cos * buf[2, r, c] - sin * buf[3, r, c]
                )
                raw = buf[4, r, c] - pred
                raw_ref[PAD + r0 : PAD + r0 + 16, c] = raw
                weighted = buf[5, r, c] * mbuf[r, c].astype(F32) * raw
                high = weighted.astype(BF16)
                split[r, c] = high
                split[R + r0 : R + r0 + 16, c] = (weighted - high.astype(F32)).astype(BF16)

    tile = lax.axis_index("tile")
    odd = tile % 2 == 1
    first = raw_ref[PAD : PAD + 1, :]
    last = raw_ref[PAD + R - 1 : PAD + R, :]
    ea_ref[...] = jnp.where(odd, first, last)
    at_end = (tile == 0) | (tile == tiles - 1)
    eb_ref[...] = jnp.where(at_end, 0.0, jnp.where(odd, last, first))

    sums = jnp.dot(split[...], gather_sum, preferred_element_type=F32)
    block_sums = ((sums[:R] + sums[R:]) * BLOCK_SCALE).astype(BF16)
    op_copy.wait()
    step = rows_all // 8
    for i in range(8):
        prod[PAD + i * step : PAD + (i + 1) * step, :] = lax.dot_general(
            opbuf[:, i * step : (i + 1) * step],
            block_sums,
            (((0,), (0,)), ((), ())),
            preferred_element_type=F32,
        )

    quarter = lax.broadcasted_iota(jnp.int32, (SUB, 128), 1) // 32

    def pack(k, carry):
        base = pl.multiple_of(k * R, 8)
        parts = [prod[pl.ds(base + SUB * g, SUB), :] for g in range(4)]
        low_half = jnp.where(quarter == 0, parts[0], parts[1])
        high_half = jnp.where(quarter == 2, parts[2], parts[3])
        packed[k] = jnp.where(quarter < 2, low_half, high_half).astype(BF16)
        return carry

    sent = []
    for n in range(tiles // SHARE):
        lax.fori_loop(n * SHARE, (n + 1) * SHARE, pack, 0, unroll=8)
        span = pl.ds(n * SHARE, SHARE)
        sent.append(pltpu.make_async_copy(packed.at[span], part_ref.at[span], out_sems.at[n]))
        sent[-1].start()
    for copy in sent:
        copy.wait()


def front(tiles, scene, table, d, v, s, o, c, m, op):
    rows_all = tiles * R
    return pl.pallas_call(
        functools.partial(front_kernel, tiles),
        out_shape=(
            pltpu.VMEM((WIN, W), F32),
            pltpu.HBM((tiles, SUB, 128), BF16),
            jax.ShapeDtypeStruct((1, W), F32),
            jax.ShapeDtypeStruct((1, W), F32),
            pltpu.VMEM((8, 128), F32),
        ),
        in_specs=[ANY] * 9,
        out_specs=(VMEM, ANY, VMEM, VMEM, VMEM),
        scratch_shapes=[
            pltpu.VMEM((6, R, W), F32),
            pltpu.VMEM((R, W), jnp.int32),
            pltpu.VMEM((R, rows_all), BF16),
            pltpu.VMEM((2 * R, W), BF16),
            pltpu.VMEM((rows_all + 2 * PAD, 128), F32),
            pltpu.VMEM((tiles, SUB, 128), BF16),
            pltpu.SMEM((1,), jnp.int32),
            pltpu.SMEM((16,), F32),
            pltpu.SemaphoreType.DMA((2, 7)),
            pltpu.SemaphoreType.DMA,
            pltpu.SemaphoreType.DMA((2,)),
            pltpu.SemaphoreType.DMA((tiles // SHARE,)),
        ],
        cost_estimate=pl.CostEstimate(flops=10**8, bytes_accessed=4 * 10**6, transcendentals=0),
        compiler_params=pltpu.CompilerParams(vmem_limit_bytes=12 * 2**20),
        name="front",
    )(scene, *map(hbm, (table, d, v, s, o, c, m, op)))


def cov_kernel(
    terms, noise, d_ref, v_ref, s_ref, cd_ref, cc_ref, nv_ref, co_ref, va_ref, cov_ref, xg_ref, we_ref
):
    interval, cos, sin = [terms[n : n + 1, 0:1] for n in range(3)]
    rows, cols = 8, 256
    across = W // cols

    def body(n, carry):
        r = pl.ds(pl.multiple_of((n // across) * rows, 8), rows)
        c = pl.ds(pl.multiple_of((n % across) * cols, 128), cols)
        x = [d_ref[0, r, c], v_ref[0, r, c], s_ref[0, 0, r, c], s_ref[1, 0, r, c]]
        diag = [cd_ref[i, 0, r, c] for i in range(4)]
        dev = [jnp.sqrt(e) for e in diag]
        p = [[None] * 4 for _ in range(4)]
        for i in range(4):
            p[i][i] = diag[i]
        for k, (i, j) in enumerate(PAIR_LIST):
            p[i][j] = p[j][i] = cc_ref[k, 0, r, c] * dev[i] * dev[j]
        q = [
            [p[0][j] + interval * p[1][j] for j in range(4)],
            [p[1][j] for j in range(4)],
            [cos * p[2][j] - sin * p[3][j] for j in range(4)],
            [sin * p[2][j] + cos * p[3][j] for j in range(4)],
        ]
        a = [[None] * 4 for _ in range(4)]
        for i in range(4):
            for j in range(i, 4):
                if j == 0:
                    e = q[i][0] + interval * q[i][1]
                elif j == 1:
                    e = q[i][1]
                elif j == 2:
                    e = cos * q[i][2] - sin * q[i][3]
                else:
                    e = sin * q[i][2] + cos * q[i][3]
                if i == j:
                    e = e + noise[i] * interval
                a[i][j] = a[j][i] = e
        pred = [
            x[0] + interval * x[1],
            x[1],
            cos * x[2] - sin * x[3],
            sin * x[2] + cos * x[3],
        ]
        coherence = co_ref[0, r, c]
        valid = va_ref[0, r, c].astype(F32)
        h = [a[i][0] + a[i][2] for i in range(4)]
        variance = h[0] + h[2] + nv_ref[0, r, c] / coherence
        scale = valid / variance
        gain = [h[i] * scale for i in range(4)]
        for i in range(4):
            xg_ref[i, r, c] = pred[i]
            xg_ref[4 + i, r, c] = gain[i]
            cov_ref[i, 0, r, c] = a[i][i] - gain[i] * h[i]
        for k, (i, j) in enumerate(PAIR_LIST):
            cov_ref[4 + k, 0, r, c] = a[i][j] - gain[i] * h[j]
        return carry

    lax.fori_loop(0, (d_ref.shape[1] // rows) * across, body, 0)
    weight = lambda c: co_ref[0, :, c : c + 128] * va_ref[0, :, c : c + 128].astype(F32)
    we_ref[:, :128] = weight(0)
    we_ref[:, 128:] = weight(W - 128)


def covariance(terms, noise, d, v, s, cd, cc, nv, co, va):
    step = 40
    plane = pl.BlockSpec((1, step, W), lambda i: (0, i, 0))
    planes = lambda n: pl.BlockSpec((n, 1, step, W), lambda i: (0, 0, i, 0))
    return pl.pallas_call(
        cov_kernel,
        grid=(R // step,),
        out_shape=(
            jax.ShapeDtypeStruct((10, 1, R, W), F32),
            pltpu.VMEM((8, R, W), F32),
            pltpu.VMEM((R, 256), F32),
        ),
        in_specs=[pl.BlockSpec((8, 128), lambda i: (0, 0)), SMEM] + [plane, plane, planes(2), planes(4), planes(6), plane, plane, plane],
        out_specs=(
            planes(10),
            pl.BlockSpec((8, step, W), lambda i: (0, i, 0)),
            pl.BlockSpec((step, 256), lambda i: (i, 0)),
        ),
        cost_estimate=pl.CostEstimate(flops=2 * 10**7, bytes_accessed=12 * 10**6, transcendentals=0),
        compiler_params=pltpu.CompilerParams(vmem_limit_bytes=24 * 2**20),
        name="covariance",
    )(vmem(terms), noise, *map(hbm, (d, v, s, cd, cc, nv, co, va)))


def clean_window(cl, screen, raw_ref, pa_ref, pb_ref, blocks):
    odd = lax.axis_index("tile") % 2 == 1
    lane = lax.broadcasted_iota(jnp.int32, (SUB, 128), 1) // 32
    for g in range(4):
        rows = slice(g * SUB, (g + 1) * SUB)
        for n, b in enumerate(blocks):
            spread = jnp.take_along_axis(screen, lane + (32 * g + 4 * b), axis=1)
            cl[rows, 128 * n : 128 * (n + 1)] = raw_ref[rows, 128 * b : 128 * (b + 1)] - spread
    above = jnp.where(odd, pa_ref[...], pb_ref[...])
    below = jnp.where(odd, pb_ref[...], pa_ref[...])
    for n, b in enumerate(blocks):
        c = slice(128 * n, 128 * (n + 1))
        o = slice(128 * b, 128 * (b + 1))
        cl[PAD - 1 : PAD, c] = cl[PAD - 1 : PAD, c] + above[:, o]
        cl[PAD + R : PAD + R + 1, c] = cl[PAD + R : PAD + R + 1, c] + below[:, o]


def smoothed(up, mid, down):
    width = mid.shape[1]
    col = lax.broadcasted_iota(jnp.int32, mid.shape, 1)
    left = jnp.where(col == 0, 0.0, pltpu.roll(mid, 1, axis=1))
    right = jnp.where(col == width - 1, 0.0, pltpu.roll(mid, width - 1, axis=1))
    return (
        mid
        + ALONG_COEF * (up + down - 2.0 * mid)
        + ACROSS_COEF * (left + right - 2.0 * mid)
    )


def picks(index_row):
    rows = lax.broadcasted_iota(jnp.int32, (R, NB), 0)
    return jnp.where(rows == (index_row >> 3), 1.0, 0.0)


def margin_kernel(
    part_ref, raw_ref, pa_ref, pb_ref, we_ref, up_ref, down_ref, screen_ref, sm_ref, ma_ref, mb_ref, cl
):
    screen = jnp.sum(part_ref[...].astype(F32), axis=0)
    screen_ref[...] = screen
    clean_window(cl, screen, raw_ref, pa_ref, pb_ref, (0, 1, 6, 7))
    smooth = smoothed(cl[PAD - 1 : PAD - 1 + R], cl[PAD : PAD + R], cl[PAD + 1 : PAD + 1 + R])
    sm_ref[:, :128] = smooth[:, :128]
    sm_ref[:, 128:] = smooth[:, 384:]
    odd = lax.axis_index("track") % 2 == 1

    def payload(index_row, weight, value):
        pick = picks(index_row).astype(BF16)
        return [
            lax.dot_general(
                pick, e.astype(BF16), (((0,), (0,)), ((), ())), preferred_element_type=F32
            )
            for e in (weight * value, weight)
        ]

    going_down = payload(down_ref[0], we_ref[:, :128], smooth[:, :128])
    going_up = payload(up_ref[0], we_ref[:, 128:], smooth[:, 384:])
    for n in range(2):
        ma_ref[n] = jnp.where(odd, going_down[n], going_up[n]).astype(BF16)
        mb_ref[n] = jnp.where(odd, going_up[n], going_down[n]).astype(BF16)


def margin(part, raw, pa, pb, we, up, down):
    return pl.pallas_call(
        margin_kernel,
        out_shape=(
            pltpu.VMEM((SUB, 128), F32),
            pltpu.VMEM((R, 256), F32),
            jax.ShapeDtypeStruct((2, NB, 128), BF16),
            jax.ShapeDtypeStruct((2, NB, 128), BF16),
        ),
        in_specs=[VMEM] * 7,
        out_specs=(VMEM,) * 4,
        scratch_shapes=[pltpu.VMEM((WIN, 512), F32)],
        cost_estimate=pl.CostEstimate(flops=10**7, bytes_accessed=10**6, transcendentals=0),
        compiler_params=pltpu.CompilerParams(vmem_limit_bytes=2 * 2**20),
        name="margin",
    )(part, vmem(raw), pa, pb, vmem(we), up, down)


def state_kernel(screen_ref, raw_ref, pa_ref, pb_ref, xg_ref, out_ref, cl, held, sems):
    clean_window(cl, screen_ref[...], raw_ref, pa_ref, pb_ref, tuple(range(8)))
    step = R // 5
    copies = []
    for n in range(5):
        r0 = n * step
        rows = slice(r0, r0 + step)
        smooth = smoothed(
            cl[PAD - 1 + r0 : PAD - 1 + r0 + step],
            cl[PAD + r0 : PAD + r0 + step],
            cl[PAD + 1 + r0 : PAD + 1 + r0 + step],
        )
        for i in range(4):
            held[i, rows] = xg_ref[i, rows] + xg_ref[4 + i, rows] * smooth
        span = pl.ds(r0, step)
        copies.append(
            pltpu.make_async_copy(held.at[:, span], out_ref.at[:, 0, span], sems.at[n])
        )
        copies[-1].start()
    for copy in copies:
        copy.wait()


def state(screen, raw, pa, pb, xg):
    return pl.pallas_call(
        state_kernel,
        out_shape=pltpu.HBM((4, 1, R, W), F32),
        in_specs=[VMEM] * 5,
        out_specs=ANY,
        scratch_shapes=[
            pltpu.VMEM((WIN, W), F32),
            pltpu.VMEM((4, R, W), F32),
            pltpu.SemaphoreType.DMA((5,)),
        ],
        cost_estimate=pl.CostEstimate(flops=2 * 10**6, bytes_accessed=4 * 10**6, transcendentals=0),
        compiler_params=pltpu.CompilerParams(vmem_limit_bytes=6 * 2**20),
        name="state",
    )(vmem(screen), vmem(raw), pa, pb, vmem(xg))


def finish_kernel(ra_ref, rb_ref, up_ref, down_ref, sm_ref, we_ref, xg_ref, _, out_ref, held, sems):
    odd = lax.axis_index("track") % 2 == 1
    a = [ra_ref[n].astype(F32) for n in range(2)]
    b = [rb_ref[n].astype(F32) for n in range(2)]
    copies = []
    for side in range(2):
        edge = slice(128 * side, 128 * side + 128)
        at = side * (W - 128)
        cols = slice(at, at + 128)
        place = picks(up_ref[0] if side else down_ref[0]).astype(BF16)
        got = []
        for n in range(2):
            mine = jnp.where(odd, b[n], a[n]) if side else jnp.where(odd, a[n], b[n])
            got.append(jnp.dot(place, mine.astype(BF16), preferred_element_type=F32))
        weight = we_ref[:, edge] + WEIGHT_FLOOR
        innovation = (weight * sm_ref[:, edge] + got[0]) / (weight + got[1])
        for i in range(4):
            held[side, i] = xg_ref[i, :, cols] + xg_ref[4 + i, :, cols] * innovation
        copies.append(
            pltpu.make_async_copy(held.at[side], out_ref.at[:, 0, :, pl.ds(at, 128)], sems.at[side])
        )
        copies[-1].start()
    for copy in copies:
        copy.wait()


def finish(ra, rb, up, down, sm, we, xg, ns):
    return pl.pallas_call(
        finish_kernel,
        out_shape=pltpu.HBM(ns.shape, F32),
        in_specs=[VMEM] * 7 + [ANY],
        out_specs=ANY,
        scratch_shapes=[pltpu.VMEM((2, 4, R, 128), F32), pltpu.SemaphoreType.DMA((2,))],
        input_output_aliases={7: 0},
        cost_estimate=pl.CostEstimate(flops=10**6, bytes_accessed=10**6, transcendentals=0),
        compiler_params=pltpu.CompilerParams(vmem_limit_bytes=3 * 2**20),
        name="finish",
    )(ra, rb, up, down, vmem(sm), vmem(we), vmem(xg), ns)


def swap(value, axis, first):
    count = lax.axis_size(axis)
    pairs = []
    for i in range(first, first + count, 2):
        a, b = i % count, (i + 1) % count
        pairs += [(a, b), (b, a)]
    return lax.ppermute(value, axis, pairs)


def local(
    displacement,
    velocity,
    seasonal,
    cov_diag,
    cov_corr,
    observed,
    noise_var,
    coherence,
    valid,
    screen_operator,
    process_noise,
    track_scene,
    scene_interval,
    margin_up,
    margin_down,
):
    tiles = lax.axis_size("tile")
    raw, part, edge_a, edge_b, terms = front(
        tiles, track_scene, scene_interval, displacement, velocity, seasonal, observed, coherence, valid, jnp.swapaxes(screen_operator, 1, 2)
    )
    part = lax.all_to_all(part, "tile", split_axis=0, concat_axis=0, tiled=True)
    near_a = swap(edge_a, "tile", 0)
    near_b = swap(edge_b, "tile", 1)
    new_cov, xg, edge_weight = covariance(
        terms,
        process_noise,
        displacement,
        velocity,
        seasonal,
        cov_diag,
        cov_corr,
        noise_var,
        coherence,
        valid,
    )
    screen, edge_smooth, out_a, out_b = margin(
        part, raw, near_a, near_b, edge_weight, margin_up, margin_down
    )
    in_b = swap(out_b, "track", 1)
    in_a = swap(out_a, "track", 0)
    new_state = state(screen, raw, near_a, near_b, xg)
    new_state = finish(in_a, in_b, margin_up, margin_down, edge_smooth, edge_weight, xg, new_state)
    return new_state, new_cov


def solution(mesh):
    in_specs = (
        P("track", "tile", None),
        P("track", "tile", None),
        P(None, "track", "tile", None),
        P(None, "track", "tile", None),
        P(None, "track", "tile", None),
        P("track", "tile", None),
        P("track", "tile", None),
        P("track", "tile", None),
        P("track", "tile", None),
        P("track", None, "tile"),
        P(),
        P("track"),
        P(),
        P("track", "tile", None),
        P("track", "tile", None),
    )
    out_specs = (P(None, "track", "tile", None), P(None, "track", "tile", None))
    return jax.shard_map(local, mesh=mesh, in_specs=in_specs, out_specs=out_specs, check_vma=False)
```

```python
import functools
import math

import jax
import jax.numpy as jnp
from jax import lax
from jax.experimental import pallas as pl
from jax.experimental.pallas import tpu as pltpu
from jax.sharding import PartitionSpec as P


SEASON_RATE = 2.0 * math.pi * 12.0 / 365.25
ALONG_COEF = 0.2
ACROSS_COEF = 0.1
WEIGHT_FLOOR = 0.1
BLOCK_SCALE = 0.25
PAIR_LIST = ((0, 1), (0, 2), (0, 3), (1, 2), (1, 3), (2, 3))

R = 80
W = 1024
PAD = 8
WIN = R + 2 * PAD
SUB = WIN // 4
NB = 40
SHARE = 16
F32 = jnp.float32
BF16 = jnp.bfloat16

SMEM = pl.BlockSpec(memory_space=pltpu.SMEM)
VMEM = pl.BlockSpec(memory_space=pltpu.VMEM)
ANY = pl.BlockSpec(memory_space=pl.ANY)


def hbm(x):
    return pltpu.with_memory_space_constraint(x, pltpu.HBM)


def vmem(x):
    return pltpu.with_memory_space_constraint(x, pltpu.VMEM)


def scene_terms(scene, table):
    interval = table[scene[0]]
    angle = jnp.full((1, 1), SEASON_RATE * interval, F32)
    return interval, jnp.cos(angle), jnp.sin(angle)


def front_kernel(
    tiles,
    scene_h,
    table_h,
    d_h,
    v_h,
    s_h,
    o_h,
    c_h,
    m_h,
    op_h,
    raw_ref,
    part_ref,
    ea_ref,
    eb_ref,
    terms_ref,
    buf,
    mbuf,
    opbuf,
    split,
    prod,
    packed,
    scene,
    table,
    sems,
    op_sem,
    scalar_sems,
    out_sems,
):
    scalar_copies = [
        pltpu.make_async_copy(scene_h, scene, scalar_sems.at[0]),
        pltpu.make_async_copy(table_h, table, scalar_sems.at[1]),
    ]
    for copy in scalar_copies:
        copy.start()
    cuts = ((0, 48), (48, 32))
    rows_all = tiles * R
    copies = []
    for i in range(2):
        rows = pl.ds(*cuts[i])
        sources = [d_h.at[0], v_h.at[0], s_h.at[0, 0], s_h.at[1, 0], o_h.at[0], c_h.at[0]]
        group = [
            pltpu.make_async_copy(src.at[rows], buf.at[n, rows], sems.at[i, n])
            for n, src in enumerate(sources)
        ]
        group.append(pltpu.make_async_copy(m_h.at[0].at[rows], mbuf.at[rows], sems.at[i, 6]))
        copies.append(group)
    for copy in copies[0]:
        copy.start()
    for copy in copies[1]:
        copy.start()
    op_copy = pltpu.make_async_copy(op_h.at[0], opbuf, op_sem)
    op_copy.start()

    col = lax.broadcasted_iota(jnp.int32, (W, 128), 0) // 32
    lane = lax.broadcasted_iota(jnp.int32, (W, 128), 1) % 32
    gather_sum = jnp.where(col == lane, 1.0, 0.0).astype(BF16)
    zeros = jnp.zeros((PAD, W), F32)
    raw_ref[0:PAD, :] = zeros
    raw_ref[PAD + R : WIN, :] = zeros
    prod[0:PAD, :] = zeros[:, :128]
    prod[PAD + rows_all : PAD + rows_all + PAD, :] = zeros[:, :128]

    for copy in scalar_copies:
        copy.wait()
    interval, cos, sin = scene_terms(scene, table)
    for n, term in enumerate((interval, cos, sin)):
        terms_ref[n : n + 1, :] = jnp.broadcast_to(term, (1, 128))
    for i in range(2):
        for copy in copies[i]:
            copy.wait()
        at, size = cuts[i]
        for r0 in range(at, at + size, 16):
            for c0 in range(0, W, 256):
                r, c = slice(r0, r0 + 16), slice(c0, c0 + 256)
                pred = (buf[0, r, c] + interval * buf[1, r, c]) + (
                    cos * buf[2, r, c] - sin * buf[3, r, c]
                )
                raw = buf[4, r, c] - pred
                raw_ref[PAD + r0 : PAD + r0 + 16, c] = raw
                weighted = buf[5, r, c] * mbuf[r, c].astype(F32) * raw
                high = weighted.astype(BF16)
                split[r, c] = high
                split[R + r0 : R + r0 + 16, c] = (weighted - high.astype(F32)).astype(BF16)

    tile = lax.axis_index("tile")
    odd = tile % 2 == 1
    first = raw_ref[PAD : PAD + 1, :]
    last = raw_ref[PAD + R - 1 : PAD + R, :]
    ea_ref[...] = jnp.where(odd, first, last)
    at_end = (tile == 0) | (tile == tiles - 1)
    eb_ref[...] = jnp.where(at_end, 0.0, jnp.where(odd, last, first))

    sums = jnp.dot(split[...], gather_sum, preferred_element_type=F32)
    block_sums = ((sums[:R] + sums[R:]) * BLOCK_SCALE).astype(BF16)
    op_copy.wait()
    step = rows_all // 8
    for i in range(8):
        prod[PAD + i * step : PAD + (i + 1) * step, :] = lax.dot_general(
            opbuf[:, i * step : (i + 1) * step],
            block_sums,
            (((0,), (0,)), ((), ())),
            preferred_element_type=F32,
        )

    quarter = lax.broadcasted_iota(jnp.int32, (SUB, 128), 1) // 32

    def pack(k, carry):
        base = pl.multiple_of(k * R, 8)
        parts = [prod[pl.ds(base + SUB * g, SUB), :] for g in range(4)]
        low_half = jnp.where(quarter == 0, parts[0], parts[1])
        high_half = jnp.where(quarter == 2, parts[2], parts[3])
        packed[k] = jnp.where(quarter < 2, low_half, high_half).astype(BF16)
        return carry

    sent = []
    for n in range(tiles // SHARE):
        lax.fori_loop(n * SHARE, (n + 1) * SHARE, pack, 0, unroll=8)
        span = pl.ds(n * SHARE, SHARE)
        sent.append(pltpu.make_async_copy(packed.at[span], part_ref.at[span], out_sems.at[n]))
        sent[-1].start()
    for copy in sent:
        copy.wait()


def front(tiles, scene, table, d, v, s, o, c, m, op):
    rows_all = tiles * R
    return pl.pallas_call(
        functools.partial(front_kernel, tiles),
        out_shape=(
            pltpu.VMEM((WIN, W), F32),
            pltpu.HBM((tiles, SUB, 128), BF16),
            jax.ShapeDtypeStruct((1, W), F32),
            jax.ShapeDtypeStruct((1, W), F32),
            pltpu.VMEM((8, 128), F32),
        ),
        in_specs=[ANY] * 9,
        out_specs=(VMEM, ANY, VMEM, VMEM, VMEM),
        scratch_shapes=[
            pltpu.VMEM((6, R, W), F32),
            pltpu.VMEM((R, W), jnp.int32),
            pltpu.VMEM((R, rows_all), BF16),
            pltpu.VMEM((2 * R, W), BF16),
            pltpu.VMEM((rows_all + 2 * PAD, 128), F32),
            pltpu.VMEM((tiles, SUB, 128), BF16),
            pltpu.SMEM((1,), jnp.int32),
            pltpu.SMEM((16,), F32),
            pltpu.SemaphoreType.DMA((2, 7)),
            pltpu.SemaphoreType.DMA,
            pltpu.SemaphoreType.DMA((2,)),
            pltpu.SemaphoreType.DMA((tiles // SHARE,)),
        ],
        cost_estimate=pl.CostEstimate(flops=10**8, bytes_accessed=4 * 10**6, transcendentals=0),
        compiler_params=pltpu.CompilerParams(vmem_limit_bytes=12 * 2**20),
        name="front",
    )(scene, *map(hbm, (table, d, v, s, o, c, m, op)))


def cov_kernel(
    terms, noise, d_ref, v_ref, s_ref, cd_ref, cc_ref, nv_ref, co_ref, va_ref, cov_ref, xg_ref, we_ref
):
    interval, cos, sin = [terms[n : n + 1, 0:1] for n in range(3)]
    rows, cols = 8, 256
    across = W // cols

    def body(n, carry):
        r = pl.ds(pl.multiple_of((n // across) * rows, 8), rows)
        c = pl.ds(pl.multiple_of((n % across) * cols, 128), cols)
        x = [d_ref[0, r, c], v_ref[0, r, c], s_ref[0, 0, r, c], s_ref[1, 0, r, c]]
        diag = [cd_ref[i, 0, r, c] for i in range(4)]
        dev = [jnp.sqrt(e) for e in diag]
        p = [[None] * 4 for _ in range(4)]
        for i in range(4):
            p[i][i] = diag[i]
        for k, (i, j) in enumerate(PAIR_LIST):
            p[i][j] = p[j][i] = cc_ref[k, 0, r, c] * dev[i] * dev[j]
        q = [
            [p[0][j] + interval * p[1][j] for j in range(4)],
            [p[1][j] for j in range(4)],
            [cos * p[2][j] - sin * p[3][j] for j in range(4)],
            [sin * p[2][j] + cos * p[3][j] for j in range(4)],
        ]
        a = [[None] * 4 for _ in range(4)]
        for i in range(4):
            for j in range(i, 4):
                if j == 0:
                    e = q[i][0] + interval * q[i][1]
                elif j == 1:
                    e = q[i][1]
                elif j == 2:
                    e = cos * q[i][2] - sin * q[i][3]
                else:
                    e = sin * q[i][2] + cos * q[i][3]
                if i == j:
                    e = e + noise[i] * interval
                a[i][j] = a[j][i] = e
        pred = [
            x[0] + interval * x[1],
            x[1],
            cos * x[2] - sin * x[3],
            sin * x[2] + cos * x[3],
        ]
        coherence = co_ref[0, r, c]
        valid = va_ref[0, r, c].astype(F32)
        h = [a[i][0] + a[i][2] for i in range(4)]
        variance = h[0] + h[2] + nv_ref[0, r, c] / coherence
        scale = valid / variance
        gain = [h[i] * scale for i in range(4)]
        for i in range(4):
            xg_ref[i, r, c] = pred[i]
            xg_ref[4 + i, r, c] = gain[i]
            cov_ref[i, 0, r, c] = a[i][i] - gain[i] * h[i]
        for k, (i, j) in enumerate(PAIR_LIST):
            cov_ref[4 + k, 0, r, c] = a[i][j] - gain[i] * h[j]
        return carry

    lax.fori_loop(0, (d_ref.shape[1] // rows) * across, body, 0)
    weight = lambda c: co_ref[0, :, c : c + 128] * va_ref[0, :, c : c + 128].astype(F32)
    we_ref[:, :128] = weight(0)
    we_ref[:, 128:] = weight(W - 128)


def covariance(terms, noise, d, v, s, cd, cc, nv, co, va):
    step = 40
    plane = pl.BlockSpec((1, step, W), lambda i: (0, i, 0))
    planes = lambda n: pl.BlockSpec((n, 1, step, W), lambda i: (0, 0, i, 0))
    return pl.pallas_call(
        cov_kernel,
        grid=(R // step,),
        out_shape=(
            jax.ShapeDtypeStruct((10, 1, R, W), F32),
            pltpu.VMEM((8, R, W), F32),
            pltpu.VMEM((R, 256), F32),
        ),
        in_specs=[pl.BlockSpec((8, 128), lambda i: (0, 0)), SMEM] + [plane, plane, planes(2), planes(4), planes(6), plane, plane, plane],
        out_specs=(
            planes(10),
            pl.BlockSpec((8, step, W), lambda i: (0, i, 0)),
            pl.BlockSpec((step, 256), lambda i: (i, 0)),
        ),
        cost_estimate=pl.CostEstimate(flops=2 * 10**7, bytes_accessed=12 * 10**6, transcendentals=0),
        compiler_params=pltpu.CompilerParams(vmem_limit_bytes=24 * 2**20),
        name="covariance",
    )(vmem(terms), noise, *map(hbm, (d, v, s, cd, cc, nv, co, va)))


def clean_window(cl, screen, raw_ref, pa_ref, pb_ref, blocks, groups=range(4)):
    odd = lax.axis_index("tile") % 2 == 1
    lane = lax.broadcasted_iota(jnp.int32, (SUB, 128), 1) // 32
    for g in groups:
        rows = slice(g * SUB, (g + 1) * SUB)
        for n, b in enumerate(blocks):
            spread = jnp.take_along_axis(screen, lane + (32 * g + 4 * b), axis=1)
            cl[rows, 128 * n : 128 * (n + 1)] = raw_ref[rows, 128 * b : 128 * (b + 1)] - spread
    above = jnp.where(odd, pa_ref[...], pb_ref[...])
    below = jnp.where(odd, pb_ref[...], pa_ref[...])
    for n, b in enumerate(blocks):
        c = slice(128 * n, 128 * (n + 1))
        o = slice(128 * b, 128 * (b + 1))
        if 0 in groups:
            cl[PAD - 1 : PAD, c] = cl[PAD - 1 : PAD, c] + above[:, o]
        if 3 in groups:
            cl[PAD + R : PAD + R + 1, c] = cl[PAD + R : PAD + R + 1, c] + below[:, o]


def smoothed(up, mid, down):
    width = mid.shape[1]
    col = lax.broadcasted_iota(jnp.int32, mid.shape, 1)
    left = jnp.where(col == 0, 0.0, pltpu.roll(mid, 1, axis=1))
    right = jnp.where(col == width - 1, 0.0, pltpu.roll(mid, width - 1, axis=1))
    return (
        mid
        + ALONG_COEF * (up + down - 2.0 * mid)
        + ACROSS_COEF * (left + right - 2.0 * mid)
    )


def picks(index_row):
    rows = lax.broadcasted_iota(jnp.int32, (R, NB), 0)
    return jnp.where(rows == (index_row >> 3), 1.0, 0.0)


def margin_kernel(
    part_ref, raw_ref, pa_ref, pb_ref, we_ref, up_ref, down_ref, screen_ref, sm_ref, ma_ref, mb_ref, cl
):
    screen = jnp.sum(part_ref[...].astype(F32), axis=0)
    screen_ref[...] = screen
    clean_window(cl, screen, raw_ref, pa_ref, pb_ref, (0, 1, 6, 7))
    smooth = smoothed(cl[PAD - 1 : PAD - 1 + R], cl[PAD : PAD + R], cl[PAD + 1 : PAD + 1 + R])
    sm_ref[:, :128] = smooth[:, :128]
    sm_ref[:, 128:] = smooth[:, 384:]
    odd = lax.axis_index("track") % 2 == 1

    def payload(index_row, weight, value):
        pick = picks(index_row).astype(BF16)
        return [
            lax.dot_general(
                pick, e.astype(BF16), (((0,), (0,)), ((), ())), preferred_element_type=F32
            )
            for e in (weight * value, weight)
        ]

    going_down = payload(down_ref[0], we_ref[:, :128], smooth[:, :128])
    going_up = payload(up_ref[0], we_ref[:, 128:], smooth[:, 384:])
    for n in range(2):
        ma_ref[n] = jnp.where(odd, going_down[n], going_up[n]).astype(BF16)
        mb_ref[n] = jnp.where(odd, going_up[n], going_down[n]).astype(BF16)


def margin(part, raw, pa, pb, we, up, down):
    return pl.pallas_call(
        margin_kernel,
        out_shape=(
            pltpu.VMEM((SUB, 128), F32),
            pltpu.VMEM((R, 256), F32),
            jax.ShapeDtypeStruct((2, NB, 128), BF16),
            jax.ShapeDtypeStruct((2, NB, 128), BF16),
        ),
        in_specs=[VMEM] * 7,
        out_specs=(VMEM,) * 4,
        scratch_shapes=[pltpu.VMEM((WIN, 512), F32)],
        cost_estimate=pl.CostEstimate(flops=10**7, bytes_accessed=10**6, transcendentals=0),
        compiler_params=pltpu.CompilerParams(vmem_limit_bytes=2 * 2**20),
        name="margin",
    )(part, vmem(raw), pa, pb, vmem(we), up, down)


def state_kernel(screen_ref, raw_ref, pa_ref, pb_ref, xg_ref, out_ref, cl, held, sems):
    screen = screen_ref[...]
    step = R // 5
    copies, cleaned = [], 0
    for n in range(5):
        r0 = n * step
        needed = min(4, (PAD + r0 + step) // SUB + 1)
        if needed > cleaned:
            groups = range(cleaned, needed)
            clean_window(cl, screen, raw_ref, pa_ref, pb_ref, tuple(range(8)), groups)
            cleaned = needed
        rows = slice(r0, r0 + step)
        smooth = smoothed(
            cl[PAD - 1 + r0 : PAD - 1 + r0 + step],
            cl[PAD + r0 : PAD + r0 + step],
            cl[PAD + 1 + r0 : PAD + 1 + r0 + step],
        )
        for i in range(4):
            held[i, rows] = xg_ref[i, rows] + xg_ref[4 + i, rows] * smooth
        span = pl.ds(r0, step)
        copies.append(
            pltpu.make_async_copy(held.at[:, span], out_ref.at[:, 0, span], sems.at[n])
        )
        copies[-1].start()
    for copy in copies:
        copy.wait()


def state(screen, raw, pa, pb, xg):
    return pl.pallas_call(
        state_kernel,
        out_shape=pltpu.HBM((4, 1, R, W), F32),
        in_specs=[VMEM] * 5,
        out_specs=ANY,
        scratch_shapes=[
            pltpu.VMEM((WIN, W), F32),
            pltpu.VMEM((4, R, W), F32),
            pltpu.SemaphoreType.DMA((5,)),
        ],
        cost_estimate=pl.CostEstimate(flops=2 * 10**6, bytes_accessed=4 * 10**6, transcendentals=0),
        compiler_params=pltpu.CompilerParams(vmem_limit_bytes=6 * 2**20),
        name="state",
    )(vmem(screen), vmem(raw), pa, pb, vmem(xg))


def finish_kernel(ra_ref, rb_ref, up_ref, down_ref, sm_ref, we_ref, xg_ref, _, out_ref, held, sems):
    odd = lax.axis_index("track") % 2 == 1
    a = [ra_ref[n].astype(F32) for n in range(2)]
    b = [rb_ref[n].astype(F32) for n in range(2)]
    copies = []
    for side in range(2):
        edge = slice(128 * side, 128 * side + 128)
        at = side * (W - 128)
        cols = slice(at, at + 128)
        place = picks(up_ref[0] if side else down_ref[0]).astype(BF16)
        got = []
        for n in range(2):
            mine = jnp.where(odd, b[n], a[n]) if side else jnp.where(odd, a[n], b[n])
            got.append(jnp.dot(place, mine.astype(BF16), preferred_element_type=F32))
        weight = we_ref[:, edge] + WEIGHT_FLOOR
        innovation = (weight * sm_ref[:, edge] + got[0]) / (weight + got[1])
        for i in range(4):
            held[side, i] = xg_ref[i, :, cols] + xg_ref[4 + i, :, cols] * innovation
        copies.append(
            pltpu.make_async_copy(held.at[side], out_ref.at[:, 0, :, pl.ds(at, 128)], sems.at[side])
        )
        copies[-1].start()
    for copy in copies:
        copy.wait()


def finish(ra, rb, up, down, sm, we, xg, ns):
    return pl.pallas_call(
        finish_kernel,
        out_shape=pltpu.HBM(ns.shape, F32),
        in_specs=[VMEM] * 7 + [ANY],
        out_specs=ANY,
        scratch_shapes=[pltpu.VMEM((2, 4, R, 128), F32), pltpu.SemaphoreType.DMA((2,))],
        input_output_aliases={7: 0},
        cost_estimate=pl.CostEstimate(flops=10**6, bytes_accessed=10**6, transcendentals=0),
        compiler_params=pltpu.CompilerParams(vmem_limit_bytes=3 * 2**20),
        name="finish",
    )(ra, rb, up, down, vmem(sm), vmem(we), vmem(xg), ns)


def swap(value, axis, first):
    count = lax.axis_size(axis)
    pairs = []
    for i in range(first, first + count, 2):
        a, b = i % count, (i + 1) % count
        pairs += [(a, b), (b, a)]
    return lax.ppermute(value, axis, pairs)


def local(
    displacement,
    velocity,
    seasonal,
    cov_diag,
    cov_corr,
    observed,
    noise_var,
    coherence,
    valid,
    screen_operator,
    process_noise,
    track_scene,
    scene_interval,
    margin_up,
    margin_down,
):
    tiles = lax.axis_size("tile")
    raw, part, edge_a, edge_b, terms = front(
        tiles, track_scene, scene_interval, displacement, velocity, seasonal, observed, coherence, valid, jnp.swapaxes(screen_operator, 1, 2)
    )
    part = lax.all_to_all(part, "tile", split_axis=0, concat_axis=0, tiled=True)
    near_a = swap(edge_a, "tile", 0)
    near_b = swap(edge_b, "tile", 1)
    new_cov, xg, edge_weight = covariance(
        terms,
        process_noise,
        displacement,
        velocity,
        seasonal,
        cov_diag,
        cov_corr,
        noise_var,
        coherence,
        valid,
    )
    screen, edge_smooth, out_a, out_b = margin(
        part, raw, near_a, near_b, edge_weight, margin_up, margin_down
    )
    in_b = swap(out_b, "track", 1)
    in_a = swap(out_a, "track", 0)
    new_state = state(screen, raw, near_a, near_b, xg)
    new_state = finish(in_a, in_b, margin_up, margin_down, edge_smooth, edge_weight, xg, new_state)
    return new_state, new_cov


def solution(mesh):
    in_specs = (
        P("track", "tile", None),
        P("track", "tile", None),
        P(None, "track", "tile", None),
        P(None, "track", "tile", None),
        P(None, "track", "tile", None),
        P("track", "tile", None),
        P("track", "tile", None),
        P("track", "tile", None),
        P("track", "tile", None),
        P("track", None, "tile"),
        P(),
        P("track"),
        P(),
        P("track", "tile", None),
        P("track", "tile", None),
    )
    out_specs = (P(None, "track", "tile", None), P(None, "track", "tile", None))
    return jax.shard_map(local, mesh=mesh, in_specs=in_specs, out_specs=out_specs, check_vma=False)
```
